128 devices in a mesh: row: 8 (over x, z_lo), col: 16 (over y, z_hi, core).
Axes of the slice: x: 4, y: 4, z: 4 (z_hi: 2, z_lo: 2; z = z_hi * 2 + z_lo), core: 2. Of those that a mesh axis runs over, the one named last changes fastest.
Arguments:
- gate_pre: bfloat16 [2048, 26624], P('col', 'row'), may hold values from -6 to 6
- up_pre: bfloat16 [2048, 26624], P('col', 'row'), may hold values from -6 to 6
- residual: bfloat16 [2048, 16384], P('row', 'col'), may hold values from -6 to 6
- base_weight: bfloat16 [26624, 16384], P('row', 'col'), may hold values from -0.0390625 to 0.0390625
- perturb: bfloat16 [26624, 16384], P('row', 'col'), may hold values from -0.0390625 to 0.0390625
- exponents: int32 [208, 16384], P('row', 'col'), may hold values from -2 to 1
Outputs:
- plus_out: bfloat16 [2048, 16384], P('row', 'col')
- minus_out: bfloat16 [2048, 16384], P('row', 'col')
The draws below stay inside these ranges and needn't reach their ends.
All inputs are finite; a program needn't handle non-finite values.
Results may differ from the reference program's by a relative error of at most 0.004.
Values may be sent and summed in bfloat16 or wider, within the bound.
A program may use at most 128 MiB of HBM per device.

```python
import jax
import jax.numpy as jnp
from jax import lax

D = 16384
FF = 26624
GROUP = 128
TOKENS = 2048
N_COL = 16


def touch_ends(array, own_key, smallest, high):
    dims = array.shape
    spot = [jax.random.randint(jax.random.fold_in(own_key, axis), (), 0, dims[axis]) for axis in range(len(dims))]
    array = array.at[tuple(spot)].set(smallest)
    longest = dims.index(max(dims))
    spot[longest] = (spot[longest] + 1) % dims[longest]
    return array.at[tuple(spot)].set(high)


def level_of(rng, extent, shards, low, high):
    gain, own = 1.0, jax.random.fold_in(rng, 6)
    for position, blocks in shards:
        steps = jnp.exp(jax.random.uniform(jax.random.fold_in(own, position), (blocks,), jnp.float32, low / len(shards), high / len(shards)))
        gain = gain * jnp.repeat(steps, extent[position] // blocks).reshape([-1 if axis == position else 1 for axis in range(len(extent))])
    return gain


def bell_draw(key, shape, spread, reach, split=(), held_as=jnp.bfloat16):
    array = spread * jax.random.normal(key, shape, jnp.float32)
    if split:
        array = array * level_of(key, shape, split, -0.22, 0.18)
    return jnp.clip(array, -reach, reach).astype(held_as)


def setup_inputs(seed: int = 0) -> dict:
    keys = jax.random.split(jax.random.key(seed), 7)
    return {
        "gate_pre": bell_draw(keys[0], (TOKENS, FF), 1.0, 6.0, ((0, 16), (1, 8))),
        "up_pre": bell_draw(keys[1], (TOKENS, FF), 1.0, 6.0, ((0, 16), (1, 8))),
        "residual": bell_draw(keys[2], (TOKENS, D), 1.0, 6.0, ((0, 8), (1, 16))),
        "base_weight": bell_draw(keys[3], (FF, D), FF ** -0.5, 0.0390625, ((0, 8), (1, 16))),
        "perturb": bell_draw(keys[4], (FF, D), FF ** -0.5, 0.0390625, ((0, 8), (1, 16))),
        "exponents": touch_ends(jax.random.randint(keys[5], (FF // GROUP, D), -2, 2), jax.random.fold_in(keys[5], 1), -2, 1).astype(jnp.int32),
    }


step_size = 0.25


def reference(gate_pre, up_pre, residual, base_weight, perturb, exponents):
    hidden = (jax.nn.silu(gate_pre.astype(jnp.float32)) * up_pre.astype(jnp.float32)).astype(jnp.bfloat16)
    columns = D // N_COL

    def column_block(block_index):
        offset = (block_index * columns).astype(jnp.int32)
        weight_block = lax.dynamic_slice_in_dim(base_weight, offset, columns, 1).astype(jnp.float32)
        direction = lax.dynamic_slice_in_dim(perturb, offset, columns, 1).astype(jnp.float32)
        powers = lax.dynamic_slice_in_dim(exponents, offset, columns, 1)
        factor = jnp.repeat(jnp.exp2(powers.astype(jnp.float32)), GROUP, axis=0)
        shift = step_size * factor * direction
        plus_weight = (weight_block + shift).astype(jnp.bfloat16)
        minus_weight = (weight_block - shift).astype(jnp.bfloat16)
        stream = lax.dynamic_slice_in_dim(residual, offset, columns, 1).astype(jnp.float32)
        plus_part = (stream + jnp.dot(hidden, plus_weight, preferred_element_type=jnp.float32)).astype(jnp.bfloat16)
        minus_part = (stream + jnp.dot(hidden, minus_weight, preferred_element_type=jnp.float32)).astype(jnp.bfloat16)
        return plus_part, minus_part

    plus_blocks, minus_blocks = lax.map(column_block, jnp.arange(N_COL, dtype=jnp.int32))
    plus_out = jnp.transpose(plus_blocks, (1, 0, 2)).reshape(TOKENS, D)
    minus_out = jnp.transpose(minus_blocks, (1, 0, 2)).reshape(TOKENS, D)
    return plus_out, minus_out
```

```python
import functools

import jax
import jax.numpy as jnp
from jax import lax
from jax.experimental import pallas as pl
from jax.experimental.pallas import tpu as pltpu
from jax.sharding import PartitionSpec as P

MESH = pl.DeviceIdType.MESH
STEP_SIZE = 0.25
CHUNKS = 4
ZP, Y_AHEAD, Y_BEHIND, OZ_AHEAD, OZ_BEHIND, Y_FAR, OZ_FAR, SIB = range(8)
N_AG = SIB + 8
FAR, MID, NEAR, ZSUM = 0, 2, 4, 6
N_RS = 7


def kernel(
    gate_hbm, up_hbm, res_ref, base_hbm, pert_hbm, expo_ref,
    plus_ref, minus_ref,
    gate_buf, up_buf, base_buf, pert_buf, factor_ref, hid, weight, part,
    far_in, mid_in, near_in, z_in,
    in_sem, w_sem, ag_send, ag_recv, rs_send, rs_recv,
):
    tokens, depth = gate_buf.shape
    piece = tokens // CHUNKS
    columns = base_buf.shape[2]
    w_rows = base_buf.shape[1]
    w_tiles = depth // w_rows
    tile_n = weight.shape[2]
    n_tiles = weight.shape[0]
    group = depth // expo_ref.shape[0]

    row, col = lax.axis_index("row"), lax.axis_index("col")
    x, zl = row // 2, row % 2
    y, zh, core = col // 4, (col // 2) % 2, col % 2
    step = 2 * core + 3
    back = 5 - 2 * core
    x_ahead, x_behind = (x + step) % 4, (x + back) % 4
    y_ahead, y_behind, y_far = (y + step) % 4, (y + back) % 4, (y + 2) % 4

    def col_of(y_, zh_, core_=core):
        return y_ * 4 + zh_ * 2 + core_

    oz, oc, ozl = 1 - zh, 1 - core, 1 - zl
    zp_dev = (row, col_of(y, oz))
    ya_dev, yb_dev = (row, col_of(y_ahead, zh)), (row, col_of(y_behind, zh))
    sib_dev = (row, col_of(y, zh, oc))
    xa_dev, xb_dev = (x_ahead * 2 + zl, col), (x_behind * 2 + zl, col)
    zl_dev = (x * 2 + ozl, col)

    origins = [
        (y, zh), (y, oz), (y_behind, zh), (y_ahead, zh),
        (y_behind, oz), (y_ahead, oz), (y_far, zh), (y_far, oz),
    ]

    in_copies = [
        pltpu.make_async_copy(gate_hbm, gate_buf, in_sem.at[0]),
        pltpu.make_async_copy(up_hbm, up_buf, in_sem.at[1]),
    ]
    for copy in in_copies:
        copy.start()

    def w_copies(i, slot):
        rows = pl.ds(pl.multiple_of(i * w_rows, w_rows), w_rows)
        return (
            pltpu.make_async_copy(base_hbm.at[rows], base_buf.at[slot], w_sem.at[0, slot]),
            pltpu.make_async_copy(pert_hbm.at[rows], pert_buf.at[slot], w_sem.at[1, slot]),
        )

    for slot in range(2):
        for copy in w_copies(slot, slot):
            copy.start()

    barrier = pltpu.get_barrier_semaphore()
    for dev in (zp_dev, ya_dev, yb_dev, sib_dev, xa_dev, xb_dev, zl_dev):
        pl.semaphore_signal(barrier, inc=1, device_id=dev, device_id_type=MESH)

    def ag(k, kind, origin, dev):
        src = hid.at[k, origin]
        return pltpu.make_async_remote_copy(
            src_ref=src, dst_ref=src, send_sem=ag_send.at[k, kind], recv_sem=ag_recv.at[k, kind],
            device_id=dev, device_id_type=MESH,
        )

    def ag_send_piece(k, kind, place, dev):
        ag(k, kind, col_of(*origins[place]), dev).start()

    def ag_wait(k, kind):
        ag(k, kind, 0, sib_dev).wait_recv()

    def to_sibling(k, place):
        ag_send_piece(k, SIB + place, place, sib_dev)

    def stage0(k):
        ag_send_piece(k, ZP, 0, zp_dev)
        ag_send_piece(k, Y_AHEAD, 0, ya_dev)
        ag_send_piece(k, Y_BEHIND, 0, yb_dev)
        to_sibling(k, 0)

    def stage1(k):
        ag_wait(k, ZP)
        ag_send_piece(k, OZ_AHEAD, 1, ya_dev)
        ag_send_piece(k, OZ_BEHIND, 1, yb_dev)
        to_sibling(k, 1)

    def stage2(k):
        ag_wait(k, Y_AHEAD)
        ag_send_piece(k, Y_FAR, 2, ya_dev)
        to_sibling(k, 2)
        ag_wait(k, Y_BEHIND)
        to_sibling(k, 3)

    def stage3(k):
        ag_wait(k, OZ_AHEAD)
        ag_send_piece(k, OZ_FAR, 4, ya_dev)
        to_sibling(k, 4)
        ag_wait(k, OZ_BEHIND)
        to_sibling(k, 5)

    def stage4(k):
        ag_wait(k, Y_FAR)
        to_sibling(k, 6)
        ag_wait(k, OZ_FAR)
        to_sibling(k, 7)

    def stage5(k):
        for place in range(8):
            ag_wait(k, SIB + place)

    def rs(k, kind, src, dst, dev):
        return pltpu.make_async_remote_copy(
            src_ref=src, dst_ref=dst, send_sem=rs_send.at[k, kind], recv_sem=rs_recv.at[k, kind],
            device_id=dev, device_id_type=MESH,
        )

    def rs_copy(k, kind):
        if kind == ZSUM:
            return rs(k, kind, part.at[k, x * 2 + ozl], z_in.at[k], zl_dev)
        lo = kind % 2
        dest, dst, dev = {
            FAR: ((x + 2) % 4, far_in, xa_dev),
            MID: (x_ahead, mid_in, xa_dev),
            NEAR: (x_behind, near_in, xb_dev),
        }[kind - lo]
        return rs(k, kind, part.at[k, dest * 2 + lo], dst.at[k, lo], dev)

    def f32(value):
        return value.astype(jnp.float32)

    def send_raw(k):
        for kind in (FAR, FAR + 1, NEAR, NEAR + 1):
            rs_copy(k, kind).start()

    def reduce_mid(k):
        for lo in range(2):
            rs_copy(k, FAR + lo).wait_recv()
            dest = x_ahead * 2 + lo
            part[k, dest] = (f32(part[k, dest]) + f32(far_in[k, lo])).astype(jnp.bfloat16)
            rs_copy(k, MID + lo).start()

    def reduce_z(k):
        for lo in range(2):
            rs_copy(k, NEAR + lo).wait_recv()
            rs_copy(k, MID + lo).wait_recv()
        dest = x * 2 + ozl
        total = f32(part[k, dest]) + f32(mid_in[k, ozl]) + f32(near_in[k, ozl])
        part[k, dest] = total.astype(jnp.bfloat16)
        rs_copy(k, ZSUM).start()

    def finish(k):
        rs_copy(k, ZSUM).wait_recv()
        for half in range(2):
            rows = pl.ds(half * piece, piece)
            out_rows = pl.ds(pl.multiple_of(half * tokens + k * piece, piece), piece)
            total = f32(part[k, x * 2 + zl, rows]) + f32(mid_in[k, zl, rows])
            total = total + f32(near_in[k, zl, rows]) + f32(z_in[k, rows])
            stream = f32(res_ref[out_rows])
            plus_ref[out_rows] = (stream + total[:, :columns]).astype(jnp.bfloat16)
            minus_ref[out_rows] = (stream + total[:, columns:]).astype(jnp.bfloat16)

    for copy in in_copies:
        copy.wait()

    def make_hidden(k):
        rows = pl.ds(pl.multiple_of(k * piece, piece), piece)
        gate, up = f32(gate_buf[rows]), f32(up_buf[rows])
        hid[k, col] = (gate / (1.0 + jnp.exp(-gate)) * up).astype(jnp.bfloat16)

    make_hidden(0)
    pl.semaphore_wait(barrier, 7)
    stage0(0)

    @pl.loop(1, CHUNKS)
    def _(k):
        make_hidden(k)

    stage0(1)
    factor_ref[...] = STEP_SIZE * jnp.exp2(expo_ref[...].astype(jnp.float32))

    @pl.loop(0, w_tiles)
    def _(i):
        slot = i % 2
        for copy in w_copies(i, slot):
            copy.wait()
        for part_group in range(w_rows // group):
            rows = pl.ds(part_group * group, group)
            factor = factor_ref[pl.ds(i * (w_rows // group) + part_group, 1)]
            base = f32(base_buf[slot, rows])
            shift = factor * f32(pert_buf[slot, rows])
            plus = (base + shift).astype(jnp.bfloat16)
            minus = (base - shift).astype(jnp.bfloat16)
            out_rows = pl.ds(pl.multiple_of(i * w_rows + part_group * group, group), group)
            for n in range(n_tiles // 2):
                cols = slice(n * tile_n, (n + 1) * tile_n)
                weight[n, out_rows] = plus[:, cols]
                weight[n + n_tiles // 2, out_rows] = minus[:, cols]

        @pl.when(i + 2 < w_tiles)
        def _():
            for copy in w_copies(i + 2, slot):
                copy.start()

        @pl.when(i == 4)
        def _():
            stage1(0)

        @pl.when(i == 6)
        def _():
            stage2(0)

        @pl.when(i == 9)
        def _():
            stage3(0)

    stage4(0)

    @pl.loop(0, CHUNKS)
    def _(k):
        stage5(k)
        more = k + 1 < CHUNKS

        @pl.loop(0, n_tiles)
        def _(n):
            lhs = hid[k].reshape(hid.shape[1] * piece, depth)
            out = jnp.dot(lhs, weight[n], preferred_element_type=jnp.float32)
            cols = pl.ds(pl.multiple_of(n * tile_n, tile_n), tile_n)
            part[k, :, :, cols] = out.astype(jnp.bfloat16).reshape(
                part.shape[1], part.shape[2], tile_n
            )

            @pl.when((n == 1) & more)
            def _():
                stage1(k + 1)

            @pl.when((n == 1) & (k + 2 < CHUNKS))
            def _():
                stage0(k + 2)

            @pl.when((n == 3) & more)
            def _():
                stage2(k + 1)

            @pl.when((n == 6) & more)
            def _():
                stage3(k + 1)

        send_raw(k)

        @pl.when(k >= 1)
        def _():
            reduce_z(k - 1)

        @pl.when(more)
        def _():
            stage4(k + 1)

        reduce_mid(k)

        @pl.when(k >= 2)
        def _():
            finish(k - 2)

    reduce_z(CHUNKS - 1)
    finish(CHUNKS - 2)
    finish(CHUNKS - 1)

    @pl.loop(0, CHUNKS)
    def _(k):
        for kind in range(N_AG):
            ag(k, kind, 0, sib_dev).wait_send()
        for kind in range(N_RS):
            rs_copy(k, kind).wait_send()


def on_device(gate_pre, up_pre, residual, base_weight, perturb, exponents):
    tokens, depth = gate_pre.shape
    columns = base_weight.shape[1]
    n_col, n_row = 16, 8
    piece = tokens // CHUNKS
    w_rows, tile_n = 256, 256
    bf16 = jnp.bfloat16
    out = jax.ShapeDtypeStruct(residual.shape, bf16)
    any_spec = pl.BlockSpec(memory_space=pl.ANY)
    vmem_spec = pl.BlockSpec(memory_space=pltpu.VMEM)
    rows_out = n_col // n_row * piece
    return pl.pallas_call(
        kernel,
        out_shape=(out, out),
        in_specs=[any_spec, any_spec, vmem_spec, any_spec, any_spec, vmem_spec],
        out_specs=(vmem_spec, vmem_spec),
        scratch_shapes=[
            pltpu.VMEM((tokens, depth), bf16),
            pltpu.VMEM((tokens, depth), bf16),
            pltpu.VMEM((2, w_rows, columns), bf16),
            pltpu.VMEM((2, w_rows, columns), bf16),
            pltpu.VMEM(exponents.shape, jnp.float32),
            pltpu.VMEM((CHUNKS, n_col, piece, depth), bf16),
            pltpu.VMEM((2 * columns // tile_n, depth, tile_n), bf16),
            pltpu.VMEM((CHUNKS, n_row, rows_out, 2 * columns), bf16),
            pltpu.VMEM((CHUNKS, 2, rows_out, 2 * columns), bf16),
            pltpu.VMEM((CHUNKS, 2, rows_out, 2 * columns), bf16),
            pltpu.VMEM((CHUNKS, 2, rows_out, 2 * columns), bf16),
            pltpu.VMEM((CHUNKS, rows_out, 2 * columns), bf16),
            pltpu.SemaphoreType.DMA((2,)),
            pltpu.SemaphoreType.DMA((2, 2)),
            pltpu.SemaphoreType.DMA((CHUNKS, N_AG)),
            pltpu.SemaphoreType.DMA((CHUNKS, N_AG)),
            pltpu.SemaphoreType.DMA((CHUNKS, N_RS)),
            pltpu.SemaphoreType.DMA((CHUNKS, N_RS)),
        ],
        compiler_params=pltpu.CompilerParams(
            collective_id=0, has_side_effects=True, vmem_limit_bytes=60 * 1024 * 1024
        ),
        cost_estimate=pl.CostEstimate(
            flops=2 * n_col * tokens * depth * 2 * columns,
            bytes_accessed=4 * depth * columns,
            transcendentals=tokens * depth,
        ),
    )(gate_pre, up_pre, residual, base_weight, perturb, exponents)


def solution(mesh):
    spec = P("row", "col")
    turned = P("col", "row")
    return jax.shard_map(
        on_device,
        mesh=mesh,
        in_specs=(turned, turned, spec, spec, spec, spec),
        out_specs=(spec, spec),
        check_vma=False,
    )
```

```python
import functools

import jax
import jax.numpy as jnp
from jax import lax
from jax.experimental import pallas as pl
from jax.experimental.pallas import tpu as pltpu
from jax.sharding import PartitionSpec as P

MESH = pl.DeviceIdType.MESH
STEP_SIZE = 0.25
CHUNKS = 8
TILE_N = 512
W_ROWS = 256
FIRST_AT = 2
NEXT_AT = 1
W_AT = (6, 10)
ZP, Y_AHEAD, Y_BEHIND, OZ_AHEAD, OZ_BEHIND, Y_FAR, OZ_FAR, SIB = range(8)
N_AG = SIB + 8
FAR, MID, NEAR, ZSUM, Z_FIRST, Z_FAR, Z_MID, Z_NEAR = 0, 2, 4, 6, 7, 8, 9, 10
N_RS = 11


def kernel(
    gate_hbm, up_hbm, res_ref, base_hbm, pert_hbm, expo_ref,
    plus_ref, minus_ref,
    gate_buf, up_buf, factor_ref, hid, weight, part,
    far_in, mid_in, near_in, z_in,
    part_z, first_in, z_far_in, z_mid_in, z_near_in,
    in_sem, w_sem, ag_send, ag_recv, rs_send, rs_recv,
):
    tokens, depth = gate_buf.shape
    piece = tokens // CHUNKS
    n_tiles, _, tile_n = weight.shape
    halves = n_tiles // 2
    columns = halves * tile_n
    w_tiles = depth // W_ROWS
    group = depth // expo_ref.shape[0]

    row, col = lax.axis_index("row"), lax.axis_index("col")
    x, zl = row // 2, row % 2
    y, zh, core = col // 4, (col // 2) % 2, col % 2
    step = 2 * core + 3
    back = 5 - 2 * core
    x_ahead, x_behind = (x + step) % 4, (x + back) % 4
    y_ahead, y_behind, y_far = (y + step) % 4, (y + back) % 4, (y + 2) % 4

    def col_of(y_, zh_, core_=core):
        return y_ * 4 + zh_ * 2 + core_

    oz, oc, ozl = 1 - zh, 1 - core, 1 - zl
    zp_dev = (row, col_of(y, oz))
    ya_dev, yb_dev = (row, col_of(y_ahead, zh)), (row, col_of(y_behind, zh))
    sib_dev = (row, col_of(y, zh, oc))
    xa_dev, xb_dev = (x_ahead * 2 + zl, col), (x_behind * 2 + zl, col)
    zl_dev = (x * 2 + ozl, col)

    origins = [
        (y, zh), (y, oz), (y_behind, zh), (y_ahead, zh),
        (y_behind, oz), (y_ahead, oz), (y_far, zh), (y_far, oz),
    ]

    in_copies = [
        pltpu.make_async_copy(gate_hbm, gate_buf, in_sem.at[0]),
        pltpu.make_async_copy(up_hbm, up_buf, in_sem.at[1]),
    ]
    for copy in in_copies:
        copy.start()

    places = ((1, 2), (3, 0))

    def w_copies(i):
        rows = pl.ds(pl.multiple_of(i * W_ROWS, W_ROWS), W_ROWS)
        copies = []
        for half in range(halves):
            cols = pl.ds(half * tile_n, tile_n)
            for j, source in enumerate((base_hbm, pert_hbm)):
                place = places[j][half]
                copies.append(pltpu.make_async_copy(
                    source.at[rows, cols], weight.at[place, rows], w_sem.at[i, place]
                ))
        return copies

    barrier = pltpu.get_barrier_semaphore()
    for dev in (zp_dev, ya_dev, yb_dev, sib_dev, xa_dev, xb_dev, zl_dev):
        pl.semaphore_signal(barrier, inc=1, device_id=dev, device_id_type=MESH)

    @pl.loop(0, w_tiles)
    def _(i):
        for copy in w_copies(i):
            copy.start()

    def ag(k, kind, origin, dev):
        src = hid.at[k, origin]
        return pltpu.make_async_remote_copy(
            src_ref=src, dst_ref=src, send_sem=ag_send.at[k, kind], recv_sem=ag_recv.at[k, kind],
            device_id=dev, device_id_type=MESH,
        )

    def ag_send_piece(k, kind, place, dev):
        ag(k, kind, col_of(*origins[place]), dev).start()

    def ag_wait(k, kind):
        ag(k, kind, 0, sib_dev).wait_recv()

    def to_sibling(k, place):
        ag_send_piece(k, SIB + place, place, sib_dev)

    def across_z(k):
        ag_send_piece(k, ZP, 0, zp_dev)

    def own_along_y(k):
        ag_send_piece(k, Y_AHEAD, 0, ya_dev)
        ag_send_piece(k, Y_BEHIND, 0, yb_dev)

    def other_along_y(k):
        ag_wait(k, ZP)
        ag_send_piece(k, OZ_AHEAD, 1, ya_dev)
        ag_send_piece(k, OZ_BEHIND, 1, yb_dev)
        to_sibling(k, 1)

    def own_onward(k):
        ag_wait(k, Y_AHEAD)
        ag_send_piece(k, Y_FAR, 2, ya_dev)
        to_sibling(k, 2)
        ag_wait(k, Y_BEHIND)
        to_sibling(k, 3)

    def other_onward(k):
        ag_wait(k, OZ_AHEAD)
        ag_send_piece(k, OZ_FAR, 4, ya_dev)
        to_sibling(k, 4)
        ag_wait(k, OZ_BEHIND)
        to_sibling(k, 5)

    def last_to_sibling(k):
        ag_wait(k, Y_FAR)
        to_sibling(k, 6)
        ag_wait(k, OZ_FAR)
        to_sibling(k, 7)

    def all_here(k):
        for place in range(8):
            ag_wait(k, SIB + place)

    def rs(k, kind, src, dst, dev):
        return pltpu.make_async_remote_copy(
            src_ref=src, dst_ref=dst, send_sem=rs_send.at[k, kind], recv_sem=rs_recv.at[k, kind],
            device_id=dev, device_id_type=MESH,
        )

    def rs_copy(k, kind):
        if kind == ZSUM:
            return rs(k, kind, part.at[k, x * 2 + ozl], z_in.at[k], zl_dev)
        if kind == Z_FIRST:
            return rs(k, kind, part_z.at[k, ozl], first_in.at[k], zl_dev)
        if kind > Z_FIRST:
            dest, dst, dev = {
                Z_FAR: ((x + 2) % 4, z_far_in, xa_dev),
                Z_MID: (x_ahead, z_mid_in, xa_dev),
                Z_NEAR: (x_behind, z_near_in, xb_dev),
            }[kind]
            return rs(k, kind, part_z.at[k, zl, dest], dst.at[k], dev)
        lo = kind % 2
        dest, dst, dev = {
            FAR: ((x + 2) % 4, far_in, xa_dev),
            MID: (x_ahead, mid_in, xa_dev),
            NEAR: (x_behind, near_in, xb_dev),
        }[kind - lo]
        return rs(k, kind, part.at[k, dest * 2 + lo], dst.at[k, lo], dev)

    def f32(value):
        return value.astype(jnp.float32)

    def send_raw(k):
        for kind in (FAR, FAR + 1, NEAR, NEAR + 1):
            rs_copy(k, kind).start()

    def pair_sum(k, dest):
        return f32(part_z[k, zl, dest]) + f32(first_in[k, dest])

    def reduce_first(k):
        rs_copy(k, Z_FIRST).wait_recv()
        for kind, dest in ((Z_FAR, (x + 2) % 4), (Z_NEAR, x_behind)):
            part_z[k, zl, dest] = pair_sum(k, dest).astype(jnp.bfloat16)
            rs_copy(k, kind).start()

    def reduce_mid(k):
        for lo in range(2):
            rs_copy(k, FAR + lo).wait_recv()
            dest = x_ahead * 2 + lo
            part[k, dest] = (f32(part[k, dest]) + f32(far_in[k, lo])).astype(jnp.bfloat16)
            rs_copy(k, MID + lo).start()
        rs_copy(k, Z_FAR).wait_recv()
        total = pair_sum(k, x_ahead) + f32(z_far_in[k])
        part_z[k, zl, x_ahead] = total.astype(jnp.bfloat16)
        rs_copy(k, Z_MID).start()

    def reduce_z(k):
        for lo in range(2):
            rs_copy(k, NEAR + lo).wait_recv()
            rs_copy(k, MID + lo).wait_recv()
        dest = x * 2 + ozl
        total = f32(part[k, dest]) + f32(mid_in[k, ozl]) + f32(near_in[k, ozl])
        part[k, dest] = total.astype(jnp.bfloat16)
        rs_copy(k, ZSUM).start()

    def finish(k):
        for kind in (ZSUM, Z_MID, Z_NEAR):
            rs_copy(k, kind).wait_recv()
        last = columns - tile_n
        for half in range(2):
            rows = pl.ds(half * piece, piece)
            out_rows = pl.ds(pl.multiple_of(half * tokens + k * piece, piece), piece)
            total = f32(part[k, x * 2 + zl, rows]) + f32(mid_in[k, zl, rows])
            total = total + f32(near_in[k, zl, rows]) + f32(z_in[k, rows])
            stream = f32(res_ref[out_rows])
            plus_ref[out_rows] = (stream + total[:, :columns]).astype(jnp.bfloat16)
            minus_ref[out_rows, :last] = (stream[:, :last] + total[:, columns:]).astype(jnp.bfloat16)
            total = f32(part_z[k, zl, x, rows]) + f32(first_in[k, x, rows])
            total = total + f32(z_mid_in[k, rows]) + f32(z_near_in[k, rows])
            minus_ref[out_rows, last:] = (stream[:, last:] + total).astype(jnp.bfloat16)

    for copy in in_copies:
        copy.wait()

    def make_hidden(k):
        rows = pl.ds(pl.multiple_of(k * piece, piece), piece)
        gate, up = f32(gate_buf[rows]), f32(up_buf[rows])
        hid[k, col] = (gate / (1.0 + jnp.exp(-gate)) * up).astype(jnp.bfloat16)

    make_hidden(0)
    pl.semaphore_wait(barrier, 7)
    across_z(0)
    own_along_y(0)
    to_sibling(0, 0)

    @pl.loop(1, CHUNKS)
    def _(k):
        make_hidden(k)
        across_z(k)
        to_sibling(k, 0)

    other_along_y(0)
    factor_ref[...] = STEP_SIZE * jnp.exp2(expo_ref[...].astype(jnp.float32))

    @pl.loop(0, w_tiles)
    def _(i):
        for copy in w_copies(i):
            copy.wait()
        for g in range(W_ROWS // group):
            rows = pl.ds(pl.multiple_of(i * W_ROWS + g * group, group), group)
            factor = factor_ref[pl.ds(i * (W_ROWS // group) + g, 1)]
            for half in range(halves):
                plus_at, minus_at = places[0][half], places[1][half]
                scale = factor[:, half * tile_n:(half + 1) * tile_n]
                base = f32(weight[plus_at, rows])
                shift = scale * f32(weight[minus_at, rows])
                weight[plus_at, rows] = (base + shift).astype(jnp.bfloat16)
                weight[minus_at, rows] = (base - shift).astype(jnp.bfloat16)

        @pl.when(i == W_AT[0])
        def _():
            own_onward(0)

        @pl.when(i == W_AT[1])
        def _():
            other_onward(0)
            own_along_y(1)
            other_along_y(1)
            own_along_y(2)

    last_to_sibling(0)

    @pl.loop(0, CHUNKS)
    def _(k):
        all_here(k)
        more = k + 1 < CHUNKS

        def product(n):
            lhs = hid[k].reshape(hid.shape[1] * piece, depth)
            out = jnp.dot(lhs, weight[n], preferred_element_type=jnp.float32)
            return out.astype(jnp.bfloat16).reshape(part.shape[1], part.shape[2], tile_n)

        out = product(0)
        for dest in range(part.shape[1]):
            part_z[k, dest % 2, dest // 2] = out[dest]
        rs_copy(k, Z_FIRST).start()

        @pl.loop(1, n_tiles)
        def _(n):
            cols = pl.ds(pl.multiple_of((n - 1) * tile_n, tile_n), tile_n)
            part[k, :, :, cols] = product(n)

            @pl.when((n == FIRST_AT) & (k == 0))
            def _():
                own_onward(1)

            @pl.when((n == jnp.where(k == 0, n_tiles - 1, NEXT_AT)) & more)
            def _():
                other_onward(k + 1)

            @pl.when((n == jnp.where(k == 0, n_tiles - 1, NEXT_AT)) & (k + 2 < CHUNKS))
            def _():
                other_along_y(k + 2)

            @pl.when((n == jnp.where(k == 0, n_tiles - 1, NEXT_AT)) & (k + 3 < CHUNKS))
            def _():
                own_along_y(k + 3)

        send_raw(k)

        @pl.when(k + 2 < CHUNKS)
        def _():
            own_onward(k + 2)

        reduce_first(k)

        @pl.when(k >= 1)
        def _():
            reduce_mid(k - 1)

        @pl.when(more)
        def _():
            last_to_sibling(k + 1)

        @pl.when(k >= 2)
        def _():
            reduce_z(k - 2)

        @pl.when(k >= 3)
        def _():
            finish(k - 3)

    reduce_mid(CHUNKS - 1)
    reduce_z(CHUNKS - 2)
    finish(CHUNKS - 3)
    reduce_z(CHUNKS - 1)
    finish(CHUNKS - 2)
    finish(CHUNKS - 1)

    @pl.loop(0, CHUNKS)
    def _(k):
        for kind in range(N_AG):
            ag(k, kind, 0, sib_dev).wait_send()
        for kind in range(N_RS):
            rs_copy(k, kind).wait_send()


def on_device(gate_pre, up_pre, residual, base_weight, perturb, exponents):
    tokens, depth = gate_pre.shape
    columns = base_weight.shape[1]
    n_col, n_row = 16, 8
    piece = tokens // CHUNKS
    bf16 = jnp.bfloat16
    out = jax.ShapeDtypeStruct(residual.shape, bf16)
    any_spec = pl.BlockSpec(memory_space=pl.ANY)
    vmem_spec = pl.BlockSpec(memory_space=pltpu.VMEM)
    wide = 2 * columns - TILE_N
    rows_out = n_col // n_row * piece
    return pl.pallas_call(
        kernel,
        out_shape=(out, out),
        in_specs=[any_spec, any_spec, vmem_spec, any_spec, any_spec, vmem_spec],
        out_specs=(vmem_spec, vmem_spec),
        scratch_shapes=[
            pltpu.VMEM((tokens, depth), bf16),
            pltpu.VMEM((tokens, depth), bf16),
            pltpu.VMEM(exponents.shape, jnp.float32),
            pltpu.VMEM((CHUNKS, n_col, piece, depth), bf16),
            pltpu.VMEM((2 * columns // TILE_N, depth, TILE_N), bf16),
            pltpu.VMEM((CHUNKS, n_row, rows_out, wide), bf16),
            pltpu.VMEM((CHUNKS, 2, rows_out, wide), bf16),
            pltpu.VMEM((CHUNKS, 2, rows_out, wide), bf16),
            pltpu.VMEM((CHUNKS, 2, rows_out, wide), bf16),
            pltpu.VMEM((CHUNKS, rows_out, wide), bf16),
            pltpu.VMEM((CHUNKS, 2, n_row // 2, rows_out, TILE_N), bf16),
            pltpu.VMEM((CHUNKS, n_row // 2, rows_out, TILE_N), bf16),
            pltpu.VMEM((CHUNKS, rows_out, TILE_N), bf16),
            pltpu.VMEM((CHUNKS, rows_out, TILE_N), bf16),
            pltpu.VMEM((CHUNKS, rows_out, TILE_N), bf16),
            pltpu.SemaphoreType.DMA((2,)),
            pltpu.SemaphoreType.DMA((depth // W_ROWS, 2 * columns // TILE_N)),
            pltpu.SemaphoreType.DMA((CHUNKS, N_AG)),
            pltpu.SemaphoreType.DMA((CHUNKS, N_AG)),
            pltpu.SemaphoreType.DMA((CHUNKS, N_RS)),
            pltpu.SemaphoreType.DMA((CHUNKS, N_RS)),
        ],
        compiler_params=pltpu.CompilerParams(
            collective_id=0, has_side_effects=True, vmem_limit_bytes=60 * 1024 * 1024
        ),
        cost_estimate=pl.CostEstimate(
            flops=2 * n_col * tokens * depth * 2 * columns,
            bytes_accessed=4 * depth * columns,
            transcendentals=tokens * depth,
        ),
    )(gate_pre, up_pre, residual, base_weight, perturb, exponents)


def solution(mesh):
    spec = P("row", "col")
    turned = P("col", "row")
    return jax.shard_map(
        on_device,
        mesh=mesh,
        in_specs=(turned, turned, spec, spec, spec, spec),
        out_specs=(spec, spec),
        check_vma=False,
    )
```

```python
import jax
import jax.numpy as jnp
from jax import lax
from jax.experimental import pallas as pl
from jax.experimental.pallas import tpu as pltpu
from jax.sharding import PartitionSpec as P

MESH = pl.DeviceIdType.MESH
STEP_SIZE = 0.25
CHUNKS = 8
X_TILES = ((0, 512), (512, 1280))
Z_TILE = (1280, 2048)
W_ROWS = 256
FIRST_AT = 1
LEAD_EARLY = True
W_AT = (8, 11)
ZP, Y_AHEAD, Y_BEHIND, Y_FAR, SIB = range(5)
FAR, MID, NEAR, ZSUM, Z_FIRST, Z_FAR, Z_MID, Z_NEAR = range(8)


def kernel(
    gate_hbm, up_hbm, res_hbm, base_hbm, pert_hbm, expo_hbm,
    plus_hbm, minus_hbm,
    gate_buf, up_buf, res_ref, expo_ref, plus_ref, minus_ref, factor_ref, hid, weight, part, part_z,
    far_in, mid_in, near_in, z_in, first_in, z_far_in, z_mid_in, z_near_in,
    in_sem, out_sem, w_sem, ag_send, ag_recv, rs_send, rs_recv,
):
    tokens, depth = gate_buf.shape
    piece = tokens // CHUNKS
    columns = weight.shape[1] // 2
    wide, wide_z = part.shape[-1], part_z.shape[-1]
    w_tiles = depth // W_ROWS
    group = depth // expo_ref.shape[0]

    row, col = lax.axis_index("row"), lax.axis_index("col")
    x, zl = row // 2, row % 2
    y, zh, core = col // 4, (col // 2) % 2, col % 2
    step = 2 * core + 3
    back = 5 - 2 * core
    x_ahead, x_behind, x_far = (x + step) % 4, (x + back) % 4, (x + 2) % 4
    y_ahead, y_behind, y_far = (y + step) % 4, (y + back) % 4, (y + 2) % 4
    oz, oc, ozl = 1 - zh, 1 - core, 1 - zl

    def col_of(y_, zh_, core_):
        return y_ * 4 + zh_ * 2 + core_

    zp_dev = (row, col_of(y, oz, core))
    ya_dev, yb_dev = (row, col_of(y_ahead, zh, core)), (row, col_of(y_behind, zh, core))
    sib_dev = (row, col_of(y, zh, oc))
    xa_dev, xb_dev = (x_ahead * 2 + zl, col), (x_behind * 2 + zl, col)
    zl_dev = (x * 2 + ozl, col)

    head, rest = pl.ds(0, piece), pl.ds(piece, tokens - piece)
    in_copies = [
        pltpu.make_async_copy(gate_hbm.at[head], gate_buf.at[head], in_sem.at[0]),
        pltpu.make_async_copy(up_hbm.at[head], up_buf.at[head], in_sem.at[1]),
        pltpu.make_async_copy(gate_hbm.at[rest], gate_buf.at[rest], in_sem.at[2]),
        pltpu.make_async_copy(up_hbm.at[rest], up_buf.at[rest], in_sem.at[3]),
        pltpu.make_async_copy(expo_hbm, expo_ref, in_sem.at[4]),
        pltpu.make_async_copy(res_hbm, res_ref, in_sem.at[5]),
    ]

    def w_copies(i):
        rows = pl.ds(pl.multiple_of(i * W_ROWS, W_ROWS), W_ROWS)
        return [
            pltpu.make_async_copy(
                source.at[rows], weight.at[rows, pl.ds(j * columns, columns)], w_sem.at[i, j]
            )
            for j, source in enumerate((base_hbm, pert_hbm))
        ]

    barrier = pltpu.get_barrier_semaphore()
    for dev in (zp_dev, ya_dev, yb_dev, sib_dev, xa_dev, xb_dev, zl_dev):
        pl.semaphore_signal(barrier, inc=1, device_id=dev, device_id_type=MESH)
    for copy in in_copies:
        copy.start()

    @pl.loop(0, w_tiles)
    def _(i):
        for copy in w_copies(i):
            copy.start()

    def ag(src, k, kind, dev):
        return pltpu.make_async_remote_copy(
            src_ref=src, dst_ref=src, send_sem=ag_send.at[kind // SIB], recv_sem=ag_recv.at[k, kind],
            device_id=dev, device_id_type=MESH,
        )

    def single(k, y_, zh_):
        return hid.at[k, core, y_ * 2 + zh_]

    def pair(k, y_):
        return hid.at[k, core, pl.ds(y_ * 2, 2)]

    def to_sibling(k, y_):
        ag(pair(k, y_), k, SIB, sib_dev).start()

    def across_z(k):
        ag(single(k, y, zh), k, ZP, zp_dev).start()

    def along_y(k):
        ag(single(k, y, oz), k, ZP, zp_dev).wait_recv()
        ag(pair(k, y), k, Y_AHEAD, ya_dev).start()
        ag(pair(k, y), k, Y_BEHIND, yb_dev).start()
        to_sibling(k, y)

    def onward(k):
        ag(pair(k, y_behind), k, Y_AHEAD, ya_dev).wait_recv()
        ag(pair(k, y_behind), k, Y_FAR, ya_dev).start()
        to_sibling(k, y_behind)
        ag(pair(k, y_ahead), k, Y_BEHIND, yb_dev).wait_recv()
        to_sibling(k, y_ahead)

    def last_to_sibling(k):
        ag(pair(k, y_far), k, Y_FAR, ya_dev).wait_recv()
        to_sibling(k, y_far)

    def all_here(k):
        ag(hid.at[k, oc], k, SIB, sib_dev).wait_recv()

    def rs_copy(k, kind):
        if kind == ZSUM:
            src, dst, dev = part.at[k, x * 2 + ozl], z_in, zl_dev
        elif kind == Z_FIRST:
            src, dst, dev = part_z.at[k, ozl], first_in, zl_dev
        elif kind > Z_FIRST:
            dest, dst, dev = {
                Z_FAR: (x_far, z_far_in, xa_dev),
                Z_MID: (x_ahead, z_mid_in, xa_dev),
                Z_NEAR: (x_behind, z_near_in, xb_dev),
            }[kind]
            src = part_z.at[k, zl, dest]
        else:
            dest, dst, dev = {
                FAR: (x_far, far_in, xa_dev),
                MID: (x_ahead, mid_in, xa_dev),
                NEAR: (x_behind, near_in, xb_dev),
            }[kind]
            src = part.at[k, pl.ds(dest * 2, 2)]
        return pltpu.make_async_remote_copy(
            src_ref=src, dst_ref=dst.at[k], send_sem=rs_send.at[kind], recv_sem=rs_recv.at[k, kind],
            device_id=dev, device_id_type=MESH,
        )

    def f32(value):
        return value.astype(jnp.float32)

    def pair_sum(k, dest):
        return f32(part_z[k, zl, dest]) + f32(first_in[k, dest])

    def reduce_first(k):
        rs_copy(k, Z_FIRST).wait_recv()
        for kind, dest in ((Z_FAR, x_far), (Z_NEAR, x_behind)):
            part_z[k, zl, dest] = pair_sum(k, dest).astype(jnp.bfloat16)
            rs_copy(k, kind).start()

    def reduce_mid(k):
        rs_copy(k, FAR).wait_recv()
        for lo in range(2):
            dest = x_ahead * 2 + lo
            part[k, dest] = (f32(part[k, dest]) + f32(far_in[k, lo])).astype(jnp.bfloat16)
        rs_copy(k, MID).start()

    def reduce_z_mid(k):
        rs_copy(k, Z_FAR).wait_recv()
        total = pair_sum(k, x_ahead) + f32(z_far_in[k])
        part_z[k, zl, x_ahead] = total.astype(jnp.bfloat16)
        rs_copy(k, Z_MID).start()

    def reduce_z(k):
        rs_copy(k, NEAR).wait_recv()
        rs_copy(k, MID).wait_recv()
        dest = x * 2 + ozl
        total = f32(part[k, dest]) + f32(mid_in[k, ozl]) + f32(near_in[k, ozl])
        part[k, dest] = total.astype(jnp.bfloat16)
        rs_copy(k, ZSUM).start()

    def finish(k):
        for kind in (Z_MID, Z_NEAR, ZSUM):
            rs_copy(k, kind).wait_recv()
        last = wide - columns
        for half in range(2):
            out_rows = pl.ds(pl.multiple_of(half * tokens + k * piece, piece), piece)
            total = f32(part[k, x * 2 + zl, half]) + f32(mid_in[k, zl, half])
            total = total + f32(near_in[k, zl, half]) + f32(z_in[k, half])
            stream = f32(res_ref[out_rows])
            plus_ref[out_rows] = (stream + total[:, :columns]).astype(jnp.bfloat16)
            minus_ref[out_rows, :last] = (stream[:, :last] + total[:, columns:]).astype(jnp.bfloat16)
            total = f32(part_z[k, zl, x, half]) + f32(first_in[k, x, half])
            total = total + f32(z_mid_in[k, half]) + f32(z_near_in[k, half])
            minus_ref[out_rows, last:] = (stream[:, last:] + total).astype(jnp.bfloat16)
        for copy in out_copies(k):
            copy.start()

    def out_copies(k):
        copies = []
        for half in range(2):
            rows = pl.ds(pl.multiple_of(half * tokens + k * piece, piece), piece)
            for j, (src, dst) in enumerate(((plus_ref, plus_hbm), (minus_ref, minus_hbm))):
                copies.append(pltpu.make_async_copy(src.at[rows], dst.at[rows], out_sem.at[k, half * 2 + j]))
        return copies

    def make_hidden(k):
        rows = pl.ds(pl.multiple_of(k * piece, piece), piece)
        gate, up = f32(gate_buf[rows]), f32(up_buf[rows])
        hid[k, core, y * 2 + zh] = (gate / (1.0 + jnp.exp(-gate)) * up).astype(jnp.bfloat16)

    for copy in in_copies[:2]:
        copy.wait()
    make_hidden(0)
    pl.semaphore_wait(barrier, 7)
    across_z(0)
    ag(single(0, y, zh), 0, Y_AHEAD, ya_dev).start()
    ag(single(0, y, zh), 0, Y_BEHIND, yb_dev).start()

    for copy in in_copies[2:4]:
        copy.wait()

    @pl.loop(1, CHUNKS)
    def _(k):
        make_hidden(k)
        across_z(k)

    ag(single(0, y, oz), 0, ZP, zp_dev).wait_recv()
    ag(single(0, y, oz), 0, Y_AHEAD, ya_dev).start()
    ag(single(0, y, oz), 0, Y_BEHIND, yb_dev).start()
    to_sibling(0, y)
    for copy in in_copies[4:]:
        copy.wait()
    factor_ref[...] = STEP_SIZE * jnp.exp2(expo_ref[...].astype(jnp.float32))

    @pl.loop(0, w_tiles)
    def _(i):
        for copy in w_copies(i):
            copy.wait()
        for g in range(W_ROWS // group):
            rows = pl.ds(pl.multiple_of(i * W_ROWS + g * group, group), group)
            factor = factor_ref[pl.ds(i * (W_ROWS // group) + g, 1)]
            left, right = slice(0, columns), slice(columns, 2 * columns)
            base = f32(weight[rows, left])
            shift = factor * f32(weight[rows, right])
            weight[rows, left] = (base + shift).astype(jnp.bfloat16)
            weight[rows, right] = (base - shift).astype(jnp.bfloat16)

        @pl.when(i == W_AT[0])
        def _():
            onward(0)
            along_y(1)

        @pl.when(i == W_AT[1])
        def _():
            if LEAD_EARLY:
                along_y(2)

    last_to_sibling(0)

    @pl.loop(0, CHUNKS)
    def _(k):
        all_here(k)
        more = k + 1 < CHUNKS

        def product(span):
            lhs = hid[k].reshape(2 * part.shape[1] * piece, depth)
            out = jnp.dot(lhs, weight[:, slice(*span)], preferred_element_type=jnp.float32)
            return out.astype(jnp.bfloat16).reshape(2, part.shape[1], piece, span[1] - span[0])

        for n, span in enumerate(X_TILES):
            out = product(span)
            for half in range(2):
                part[k, :, half, :, slice(*span)] = out[half]

            if n == FIRST_AT:
                @pl.when(k == 0)
                def _():
                    onward(1)
                    along_y(3)

        rs_copy(k, FAR).start()
        rs_copy(k, NEAR).start()
        out = product(Z_TILE)
        for half in range(2):
            for dest in range(part.shape[1]):
                part_z[k, dest % 2, dest // 2, half] = out[half, dest]
        rs_copy(k, Z_FIRST).start()

        @pl.when(k >= 1)
        def _():
            reduce_first(k - 1)

        @pl.when(k + 2 < CHUNKS)
        def _():
            onward(k + 2)

        @pl.when(k + 4 < CHUNKS)
        def _():
            along_y(k + 4)

        @pl.when(more)
        def _():
            last_to_sibling(k + 1)

        @pl.when(k >= 1)
        def _():
            reduce_mid(k - 1)

        @pl.when(k >= 2)
        def _():
            reduce_z_mid(k - 2)
            reduce_z(k - 2)

        @pl.when(k >= 3)
        def _():
            finish(k - 3)

    reduce_z_mid(CHUNKS - 2)
    reduce_mid(CHUNKS - 1)
    reduce_first(CHUNKS - 1)
    reduce_z(CHUNKS - 2)
    finish(CHUNKS - 3)
    reduce_z_mid(CHUNKS - 1)
    reduce_z(CHUNKS - 1)
    finish(CHUNKS - 2)
    finish(CHUNKS - 1)

    @pl.loop(0, CHUNKS)
    def _(k):
        for copy in out_copies(k):
            copy.wait()

    def sent(src, sem):
        pltpu.make_async_remote_copy(
            src_ref=src, dst_ref=src, send_sem=sem, recv_sem=ag_recv.at[0, 0],
            device_id=sib_dev, device_id_type=MESH,
        ).wait_send()

    sent(hid.at[:, 0, pl.ds(0, 7)], ag_send.at[0])
    sent(hid.at[:, 0], ag_send.at[1])
    for kind in (FAR, MID, NEAR):
        sent(part.at[:, pl.ds(0, 2)], rs_send.at[kind])
    sent(part.at[:, 0], rs_send.at[ZSUM])
    sent(part_z.at[:, 0], rs_send.at[Z_FIRST])
    for kind in (Z_FAR, Z_MID, Z_NEAR):
        sent(part_z.at[:, 0, 0], rs_send.at[kind])


def on_device(gate_pre, up_pre, residual, base_weight, perturb, exponents):
    tokens, depth = gate_pre.shape
    columns = base_weight.shape[1]
    n_col, n_row = 16, 8
    piece = tokens // CHUNKS
    wide, wide_z = Z_TILE[0], Z_TILE[1] - Z_TILE[0]
    bf16 = jnp.bfloat16
    out = jax.ShapeDtypeStruct(residual.shape, bf16)
    any_spec = pl.BlockSpec(memory_space=pl.ANY)
    block, block_z = (2, piece, wide), (2, piece, wide_z)
    return pl.pallas_call(
        kernel,
        out_shape=(out, out),
        in_specs=[any_spec] * 6,
        out_specs=(any_spec, any_spec),
        scratch_shapes=[
            pltpu.VMEM((tokens, depth), bf16),
            pltpu.VMEM((tokens, depth), bf16),
            pltpu.VMEM(residual.shape, bf16),
            pltpu.VMEM(exponents.shape, jnp.int32),
            pltpu.VMEM(residual.shape, bf16),
            pltpu.VMEM(residual.shape, bf16),
            pltpu.VMEM(exponents.shape, jnp.float32),
            pltpu.VMEM((CHUNKS, 2, n_col // 2, piece, depth), bf16),
            pltpu.VMEM((depth, 2 * columns), bf16),
            pltpu.VMEM((CHUNKS, n_row, *block), bf16),
            pltpu.VMEM((CHUNKS, 2, n_row // 2, *block_z), bf16),
            pltpu.VMEM((CHUNKS, 2, *block), bf16),
            pltpu.VMEM((CHUNKS, 2, *block), bf16),
            pltpu.VMEM((CHUNKS, 2, *block), bf16),
            pltpu.VMEM((CHUNKS, *block), bf16),
            pltpu.VMEM((CHUNKS, n_row // 2, *block_z), bf16),
            pltpu.VMEM((CHUNKS, *block_z), bf16),
            pltpu.VMEM((CHUNKS, *block_z), bf16),
            pltpu.VMEM((CHUNKS, *block_z), bf16),
            pltpu.SemaphoreType.DMA((6,)),
            pltpu.SemaphoreType.DMA((CHUNKS, 4)),
            pltpu.SemaphoreType.DMA((depth // W_ROWS, 2)),
            pltpu.SemaphoreType.DMA((2,)),
            pltpu.SemaphoreType.DMA((CHUNKS, 5)),
            pltpu.SemaphoreType.DMA((8,)),
            pltpu.SemaphoreType.DMA((CHUNKS, 8)),
        ],
        compiler_params=pltpu.CompilerParams(
            collective_id=0, has_side_effects=True, vmem_limit_bytes=60 * 1024 * 1024
        ),
        cost_estimate=pl.CostEstimate(
            flops=2 * n_col * tokens * depth * 2 * columns,
            bytes_accessed=4 * depth * columns,
            transcendentals=tokens * depth,
        ),
    )(gate_pre, up_pre, residual, base_weight, perturb, exponents)


def solution(mesh):
    spec = P("row", "col")
    turned = P("col", "row")
    return jax.shard_map(
        on_device,
        mesh=mesh,
        in_specs=(turned, turned, spec, spec, spec, spec),
        out_specs=(spec, spec),
        check_vma=False,
    )
```

```python
import jax
import jax.numpy as jnp
from jax import lax
from jax.experimental import pallas as pl
from jax.experimental.pallas import tpu as pltpu
from jax.sharding import PartitionSpec as P

MESH = pl.DeviceIdType.MESH
STEP_SIZE = 0.25
CHUNKS = 8
X_TILES = ((0, 512), (512, 1152))
Z_TILE = (1152, 2048)
W_ROWS = 256
FIRST_AT = 1
LEAD_EARLY = True
W_AT = (8, 11)
ZP, Y_AHEAD, Y_BEHIND, Y_FAR, SIB = range(5)
FAR, MID, NEAR, ZSUM, Z_FIRST, Z_FAR, Z_MID, Z_NEAR = range(8)


def kernel(
    gate_hbm, up_hbm, res_hbm, base_hbm, pert_hbm, expo_hbm,
    out_hbm,
    gate_buf, up_buf, res_ref, expo_ref, out_ref, factor_ref, hid, weight, part, part_z,
    far_in, mid_in, near_in, z_in, first_in, z_far_in, z_mid_in, z_near_in,
    in_sem, out_sem, w_sem, ag_send, ag_recv, rs_send, rs_recv,
):
    tokens, depth = gate_buf.shape
    piece = tokens // CHUNKS
    columns = weight.shape[1] // 2
    wide, wide_z = part.shape[-1], part_z.shape[-1]
    w_tiles = depth // W_ROWS
    group = depth // expo_ref.shape[0]

    row, col = lax.axis_index("row"), lax.axis_index("col")
    x, zl = row // 2, row % 2
    y, zh, core = col // 4, (col // 2) % 2, col % 2
    step = 2 * core + 3
    back = 5 - 2 * core
    x_ahead, x_behind, x_far = (x + step) % 4, (x + back) % 4, (x + 2) % 4
    y_ahead, y_behind, y_far = (y + step) % 4, (y + back) % 4, (y + 2) % 4
    oz, oc, ozl = 1 - zh, 1 - core, 1 - zl

    def col_of(y_, zh_, core_):
        return y_ * 4 + zh_ * 2 + core_

    zp_dev = (row, col_of(y, oz, core))
    ya_dev, yb_dev = (row, col_of(y_ahead, zh, core)), (row, col_of(y_behind, zh, core))
    sib_dev = (row, col_of(y, zh, oc))
    xa_dev, xb_dev = (x_ahead * 2 + zl, col), (x_behind * 2 + zl, col)
    zl_dev = (x * 2 + ozl, col)

    head, rest = pl.ds(0, piece), pl.ds(piece, tokens - piece)
    in_copies = [
        pltpu.make_async_copy(gate_hbm.at[head], gate_buf.at[head], in_sem.at[0]),
        pltpu.make_async_copy(up_hbm.at[head], up_buf.at[head], in_sem.at[1]),
        pltpu.make_async_copy(gate_hbm.at[rest], gate_buf.at[rest], in_sem.at[2]),
        pltpu.make_async_copy(up_hbm.at[rest], up_buf.at[rest], in_sem.at[3]),
        pltpu.make_async_copy(expo_hbm, expo_ref, in_sem.at[4]),
        pltpu.make_async_copy(res_hbm, res_ref, in_sem.at[5]),
    ]

    def w_copies(i):
        rows = pl.ds(pl.multiple_of(i * W_ROWS, W_ROWS), W_ROWS)
        return [
            pltpu.make_async_copy(
                source.at[rows], weight.at[rows, pl.ds(j * columns, columns)], w_sem.at[i, j]
            )
            for j, source in enumerate((base_hbm, pert_hbm))
        ]

    barrier = pltpu.get_barrier_semaphore()
    for dev in (zp_dev, ya_dev, yb_dev, sib_dev, xa_dev, xb_dev, zl_dev):
        pl.semaphore_signal(barrier, inc=1, device_id=dev, device_id_type=MESH)
    for copy in in_copies:
        copy.start()

    @pl.loop(0, w_tiles)
    def _(i):
        for copy in w_copies(i):
            copy.start()

    def ag(src, k, kind, dev):
        return pltpu.make_async_remote_copy(
            src_ref=src, dst_ref=src, send_sem=ag_send.at[kind // SIB], recv_sem=ag_recv.at[k, kind],
            device_id=dev, device_id_type=MESH,
        )

    def single(k, y_, zh_):
        return hid.at[k, core, y_ * 2 + zh_]

    def pair(k, y_):
        return hid.at[k, core, pl.ds(y_ * 2, 2)]

    def to_sibling(k, y_):
        ag(pair(k, y_), k, SIB, sib_dev).start()

    def across_z(k):
        ag(single(k, y, zh), k, ZP, zp_dev).start()

    def along_y(k):
        ag(single(k, y, oz), k, ZP, zp_dev).wait_recv()
        ag(pair(k, y), k, Y_AHEAD, ya_dev).start()
        ag(pair(k, y), k, Y_BEHIND, yb_dev).start()
        to_sibling(k, y)

    def onward(k):
        ag(pair(k, y_behind), k, Y_AHEAD, ya_dev).wait_recv()
        ag(pair(k, y_behind), k, Y_FAR, ya_dev).start()
        to_sibling(k, y_behind)
        ag(pair(k, y_ahead), k, Y_BEHIND, yb_dev).wait_recv()
        to_sibling(k, y_ahead)

    def last_to_sibling(k):
        ag(pair(k, y_far), k, Y_FAR, ya_dev).wait_recv()
        to_sibling(k, y_far)

    def all_here(k):
        ag(hid.at[k, oc], k, SIB, sib_dev).wait_recv()

    def rs_copy(k, kind):
        if kind == ZSUM:
            src, dst, dev = part.at[k, x * 2 + ozl], z_in, zl_dev
        elif kind == Z_FIRST:
            src, dst, dev = part_z.at[k, ozl], first_in, zl_dev
        elif kind > Z_FIRST:
            dest, dst, dev = {
                Z_FAR: (x_far, z_far_in, xa_dev),
                Z_MID: (x_ahead, z_mid_in, xa_dev),
                Z_NEAR: (x_behind, z_near_in, xb_dev),
            }[kind]
            src = part_z.at[k, zl, dest]
        else:
            dest, dst, dev = {
                FAR: (x_far, far_in, xa_dev),
                MID: (x_ahead, mid_in, xa_dev),
                NEAR: (x_behind, near_in, xb_dev),
            }[kind]
            src = part.at[k, pl.ds(dest * 2, 2)]
        return pltpu.make_async_remote_copy(
            src_ref=src, dst_ref=dst.at[k], send_sem=rs_send.at[kind], recv_sem=rs_recv.at[k, kind],
            device_id=dev, device_id_type=MESH,
        )

    def f32(value):
        return value.astype(jnp.float32)

    def pair_sum(k, dest):
        return f32(part_z[k, zl, dest]) + f32(first_in[k, dest])

    def reduce_first(k):
        rs_copy(k, Z_FIRST).wait_recv()
        for kind, dest in ((Z_FAR, x_far), (Z_NEAR, x_behind)):
            part_z[k, zl, dest] = pair_sum(k, dest).astype(jnp.bfloat16)
            rs_copy(k, kind).start()

    def reduce_mid(k):
        rs_copy(k, FAR).wait_recv()
        for lo in range(2):
            dest = x_ahead * 2 + lo
            part[k, dest] = (f32(part[k, dest]) + f32(far_in[k, lo])).astype(jnp.bfloat16)
        rs_copy(k, MID).start()

    def reduce_z_mid(k):
        rs_copy(k, Z_FAR).wait_recv()
        total = pair_sum(k, x_ahead) + f32(z_far_in[k])
        part_z[k, zl, x_ahead] = total.astype(jnp.bfloat16)
        rs_copy(k, Z_MID).start()

    def reduce_z(k):
        rs_copy(k, NEAR).wait_recv()
        rs_copy(k, MID).wait_recv()
        dest = x * 2 + ozl
        total = f32(part[k, dest]) + f32(mid_in[k, ozl]) + f32(near_in[k, ozl])
        part[k, dest] = total.astype(jnp.bfloat16)
        rs_copy(k, ZSUM).start()

    def finish(k):
        for kind in (Z_MID, Z_NEAR, ZSUM):
            rs_copy(k, kind).wait_recv()
        last = wide - columns
        for half in range(2):
            out_rows = pl.ds(pl.multiple_of(half * tokens + k * piece, piece), piece)
            total = f32(part[k, x * 2 + zl, half]) + f32(mid_in[k, zl, half])
            total = total + f32(near_in[k, zl, half]) + f32(z_in[k, half])
            stream = f32(res_ref[out_rows])
            out_ref[out_rows, :columns] = (stream + total[:, :columns]).astype(jnp.bfloat16)
            out_ref[out_rows, columns:wide] = (stream[:, :last] + total[:, columns:]).astype(jnp.bfloat16)
            total = f32(part_z[k, zl, x, half]) + f32(first_in[k, x, half])
            total = total + f32(z_mid_in[k, half]) + f32(z_near_in[k, half])
            out_ref[out_rows, wide:] = (stream[:, last:] + total).astype(jnp.bfloat16)
        for copy in out_copies(k):
            copy.start()

    def out_copies(k):
        copies = []
        for half in range(2):
            rows = pl.ds(pl.multiple_of(half * tokens + k * piece, piece), piece)
            copies.append(pltpu.make_async_copy(out_ref.at[rows], out_hbm.at[rows], out_sem.at[k, half]))
        return copies

    def make_hidden(k):
        rows = pl.ds(pl.multiple_of(k * piece, piece), piece)
        gate, up = f32(gate_buf[rows]), f32(up_buf[rows])
        hid[k, core, y * 2 + zh] = (gate / (1.0 + jnp.exp(-gate)) * up).astype(jnp.bfloat16)

    for copy in in_copies[:2]:
        copy.wait()
    make_hidden(0)
    pl.semaphore_wait(barrier, 7)
    across_z(0)
    ag(single(0, y, zh), 0, Y_AHEAD, ya_dev).start()
    ag(single(0, y, zh), 0, Y_BEHIND, yb_dev).start()

    for copy in in_copies[2:4]:
        copy.wait()

    @pl.loop(1, CHUNKS)
    def _(k):
        make_hidden(k)
        across_z(k)

    ag(single(0, y, oz), 0, ZP, zp_dev).wait_recv()
    ag(single(0, y, oz), 0, Y_AHEAD, ya_dev).start()
    ag(single(0, y, oz), 0, Y_BEHIND, yb_dev).start()
    to_sibling(0, y)
    for copy in in_copies[4:]:
        copy.wait()
    factor_ref[...] = STEP_SIZE * jnp.exp2(expo_ref[...].astype(jnp.float32))

    @pl.loop(0, w_tiles)
    def _(i):
        for copy in w_copies(i):
            copy.wait()
        for g in range(W_ROWS // group):
            rows = pl.ds(pl.multiple_of(i * W_ROWS + g * group, group), group)
            factor = factor_ref[pl.ds(i * (W_ROWS // group) + g, 1)]
            left, right = slice(0, columns), slice(columns, 2 * columns)
            base = f32(weight[rows, left])
            shift = factor * f32(weight[rows, right])
            weight[rows, left] = (base + shift).astype(jnp.bfloat16)
            weight[rows, right] = (base - shift).astype(jnp.bfloat16)

        @pl.when(i == W_AT[0])
        def _():
            onward(0)
            along_y(1)

        @pl.when(i == W_AT[1])
        def _():
            if LEAD_EARLY:
                along_y(2)

    last_to_sibling(0)

    @pl.loop(0, CHUNKS)
    def _(k):
        all_here(k)
        more = k + 1 < CHUNKS

        def product(span):
            lhs = hid[k].reshape(2 * part.shape[1] * piece, depth)
            out = jnp.dot(lhs, weight[:, slice(*span)], preferred_element_type=jnp.float32)
            return out.astype(jnp.bfloat16).reshape(2, part.shape[1], piece, span[1] - span[0])

        for n, span in enumerate(X_TILES):
            out = product(span)
            for half in range(2):
                part[k, :, half, :, slice(*span)] = out[half]

            if n == FIRST_AT:
                @pl.when(k == 0)
                def _():
                    onward(1)
                    along_y(3)

        rs_copy(k, FAR).start()
        rs_copy(k, NEAR).start()
        @pl.when(k + 2 < CHUNKS)
        def _():
            onward(k + 2)

        @pl.when(k + 4 < CHUNKS)
        def _():
            along_y(k + 4)

        out = product(Z_TILE)
        for half in range(2):
            for dest in range(part.shape[1]):
                part_z[k, dest % 2, dest // 2, half] = out[half, dest]
        rs_copy(k, Z_FIRST).start()

        @pl.when(k >= 1)
        def _():
            reduce_first(k - 1)

        @pl.when(more)
        def _():
            last_to_sibling(k + 1)

        @pl.when(k >= 1)
        def _():
            reduce_mid(k - 1)

        @pl.when(k >= 2)
        def _():
            reduce_z_mid(k - 2)
            reduce_z(k - 2)

        @pl.when(k >= 3)
        def _():
            finish(k - 3)

    reduce_mid(CHUNKS - 1)
    reduce_z_mid(CHUNKS - 2)
    reduce_z(CHUNKS - 2)
    reduce_first(CHUNKS - 1)
    finish(CHUNKS - 3)
    reduce_z(CHUNKS - 1)
    reduce_z_mid(CHUNKS - 1)
    finish(CHUNKS - 2)
    finish(CHUNKS - 1)

    @pl.loop(0, CHUNKS)
    def _(k):
        for copy in out_copies(k):
            copy.wait()

    def sent(src, sem):
        pltpu.make_async_remote_copy(
            src_ref=src, dst_ref=src, send_sem=sem, recv_sem=ag_recv.at[0, 0],
            device_id=sib_dev, device_id_type=MESH,
        ).wait_send()

    sent(hid.at[:, 0, pl.ds(0, 7)], ag_send.at[0])
    sent(hid.at[:, 0], ag_send.at[1])
    for kind in (FAR, MID, NEAR):
        sent(part.at[:, pl.ds(0, 2)], rs_send.at[kind])
    sent(part.at[:, 0], rs_send.at[ZSUM])
    sent(part_z.at[:, 0], rs_send.at[Z_FIRST])
    for kind in (Z_FAR, Z_MID, Z_NEAR):
        sent(part_z.at[:, 0, 0], rs_send.at[kind])


def on_device(gate_pre, up_pre, residual, base_weight, perturb, exponents):
    tokens, depth = gate_pre.shape
    columns = base_weight.shape[1]
    n_col, n_row = 16, 8
    piece = tokens // CHUNKS
    wide, wide_z = Z_TILE[0], Z_TILE[1] - Z_TILE[0]
    bf16 = jnp.bfloat16
    out = jax.ShapeDtypeStruct((residual.shape[0], 2 * columns), bf16)
    any_spec = pl.BlockSpec(memory_space=pl.ANY)
    block, block_z = (2, piece, wide), (2, piece, wide_z)
    both = pl.pallas_call(
        kernel,
        out_shape=out,
        in_specs=[any_spec] * 6,
        out_specs=any_spec,
        scratch_shapes=[
            pltpu.VMEM((tokens, depth), bf16),
            pltpu.VMEM((tokens, depth), bf16),
            pltpu.VMEM(residual.shape, bf16),
            pltpu.VMEM(exponents.shape, jnp.int32),
            pltpu.VMEM(out.shape, bf16),
            pltpu.VMEM(exponents.shape, jnp.float32),
            pltpu.VMEM((CHUNKS, 2, n_col // 2, piece, depth), bf16),
            pltpu.VMEM((depth, 2 * columns), bf16),
            pltpu.VMEM((CHUNKS, n_row, *block), bf16),
            pltpu.VMEM((CHUNKS, 2, n_row // 2, *block_z), bf16),
            pltpu.VMEM((CHUNKS, 2, *block), bf16),
            pltpu.VMEM((CHUNKS, 2, *block), bf16),
            pltpu.VMEM((CHUNKS, 2, *block), bf16),
            pltpu.VMEM((CHUNKS, *block), bf16),
            pltpu.VMEM((CHUNKS, n_row // 2, *block_z), bf16),
            pltpu.VMEM((CHUNKS, *block_z), bf16),
            pltpu.VMEM((CHUNKS, *block_z), bf16),
            pltpu.VMEM((CHUNKS, *block_z), bf16),
            pltpu.SemaphoreType.DMA((6,)),
            pltpu.SemaphoreType.DMA((CHUNKS, 2)),
            pltpu.SemaphoreType.DMA((depth // W_ROWS, 2)),
            pltpu.SemaphoreType.DMA((2,)),
            pltpu.SemaphoreType.DMA((CHUNKS, 5)),
            pltpu.SemaphoreType.DMA((8,)),
            pltpu.SemaphoreType.DMA((CHUNKS, 8)),
        ],
        compiler_params=pltpu.CompilerParams(
            collective_id=0, has_side_effects=True, vmem_limit_bytes=60 * 1024 * 1024
        ),
        cost_estimate=pl.CostEstimate(
            flops=2 * n_col * tokens * depth * 2 * columns,
            bytes_accessed=4 * depth * columns,
            transcendentals=tokens * depth,
        ),
    )(gate_pre, up_pre, residual, base_weight, perturb, exponents)
    return both[:, :columns], both[:, columns:]


def solution(mesh):
    spec = P("row", "col")
    turned = P("col", "row")
    return jax.shard_map(
        on_device,
        mesh=mesh,
        in_specs=(turned, turned, spec, spec, spec, spec),
        out_specs=(spec, spec),
        check_vma=False,
    )
```

```python
import jax
import jax.numpy as jnp
from jax import lax
from jax.experimental import pallas as pl
from jax.experimental.pallas import tpu as pltpu
from jax.sharding import PartitionSpec as P

MESH = pl.DeviceIdType.MESH
STEP_SIZE = 0.25
CHUNKS = 8
X_TILES = ((0, 512), (512, 1152))
Z_TILE = (1152, 2048)
W_ROWS = 256
FIRST_AT = 0
W_AT = (5, 9)
ZP, Y_AHEAD, Y_BEHIND, Y_FAR, SIB, FIRST_OTHER = range(6)
FAR, MID, NEAR, ZSUM, Z_FIRST, Z_FAR, Z_MID, Z_NEAR = range(8)


def kernel(
    gate_hbm, up_hbm, res_hbm, base_hbm, pert_hbm, expo_hbm,
    out_hbm,
    gate_buf, up_buf, res_ref, expo_ref, out_ref, factor_ref, hid, weight, part, part_z,
    far_in, mid_in, near_in, z_in, first_in, z_far_in, z_mid_in, z_near_in,
    in_sem, out_sem, w_sem, ag_send, ag_recv, rs_send, rs_recv,
):
    tokens, depth = gate_buf.shape
    piece = tokens // CHUNKS
    columns = weight.shape[1] // 2
    wide, wide_z = part.shape[-1], part_z.shape[-1]
    w_tiles = depth // W_ROWS
    group = depth // expo_ref.shape[0]

    row, col = lax.axis_index("row"), lax.axis_index("col")
    x, zl = row // 2, row % 2
    y, zh, core = col // 4, (col // 2) % 2, col % 2
    step = 2 * core + 3
    back = 5 - 2 * core
    x_ahead, x_behind, x_far = (x + step) % 4, (x + back) % 4, (x + 2) % 4
    y_ahead, y_behind, y_far = (y + step) % 4, (y + back) % 4, (y + 2) % 4
    oz, oc, ozl = 1 - zh, 1 - core, 1 - zl

    def col_of(y_, zh_, core_):
        return y_ * 4 + zh_ * 2 + core_

    zp_dev = (row, col_of(y, oz, core))
    ya_dev, yb_dev = (row, col_of(y_ahead, zh, core)), (row, col_of(y_behind, zh, core))
    sib_dev = (row, col_of(y, zh, oc))
    xa_dev, xb_dev = (x_ahead * 2 + zl, col), (x_behind * 2 + zl, col)
    zl_dev = (x * 2 + ozl, col)

    head, rest = pl.ds(0, piece), pl.ds(piece, tokens - piece)
    in_copies = [
        pltpu.make_async_copy(gate_hbm.at[head], gate_buf.at[head], in_sem.at[0]),
        pltpu.make_async_copy(up_hbm.at[head], up_buf.at[head], in_sem.at[1]),
        pltpu.make_async_copy(gate_hbm.at[rest], gate_buf.at[rest], in_sem.at[2]),
        pltpu.make_async_copy(up_hbm.at[rest], up_buf.at[rest], in_sem.at[3]),
        pltpu.make_async_copy(expo_hbm, expo_ref, in_sem.at[4]),
        pltpu.make_async_copy(res_hbm, res_ref, in_sem.at[5]),
    ]

    def w_copies(i):
        rows = pl.ds(pl.multiple_of(i * W_ROWS, W_ROWS), W_ROWS)
        return [
            pltpu.make_async_copy(
                source.at[rows], weight.at[rows, pl.ds(j * columns, columns)], w_sem.at[i, j]
            )
            for j, source in enumerate((base_hbm, pert_hbm))
        ]

    barrier = pltpu.get_barrier_semaphore()
    for dev in (zp_dev, ya_dev, yb_dev, sib_dev, xa_dev, xb_dev, zl_dev):
        pl.semaphore_signal(barrier, inc=1, device_id=dev, device_id_type=MESH)
    for copy in in_copies:
        copy.start()

    @pl.loop(0, w_tiles)
    def _(i):
        for copy in w_copies(i):
            copy.start()

    def ag(src, k, kind, dev):
        return pltpu.make_async_remote_copy(
            src_ref=src, dst_ref=src, send_sem=ag_send.at[kind == SIB and 1 or 0], recv_sem=ag_recv.at[k, kind],
            device_id=dev, device_id_type=MESH,
        )

    def single(k, y_, zh_):
        return hid.at[k, core, y_ * 2 + zh_]

    def pair(k, y_):
        return hid.at[k, core, pl.ds(y_ * 2, 2)]

    def to_sibling(k, y_):
        ag(pair(k, y_), k, SIB, sib_dev).start()

    def across_z(k):
        ag(single(k, y, zh), k, ZP, zp_dev).start()

    def along_y(k):
        ag(single(k, y, oz), k, ZP, zp_dev).wait_recv()
        ag(pair(k, y), k, Y_AHEAD, ya_dev).start()
        ag(pair(k, y), k, Y_BEHIND, yb_dev).start()
        to_sibling(k, y)

    def onward(k):
        ag(pair(k, y_behind), k, Y_AHEAD, ya_dev).wait_recv()
        ag(pair(k, y_behind), k, Y_FAR, ya_dev).start()
        to_sibling(k, y_behind)
        ag(pair(k, y_ahead), k, Y_BEHIND, yb_dev).wait_recv()
        to_sibling(k, y_ahead)

    def last_to_sibling(k):
        ag(pair(k, y_far), k, Y_FAR, ya_dev).wait_recv()
        to_sibling(k, y_far)

    def all_here(k):
        ag(hid.at[k, oc], k, SIB, sib_dev).wait_recv()

    def rs_copy(k, kind):
        if kind == ZSUM:
            src, dst, dev = part.at[k, x * 2 + ozl], z_in, zl_dev
        elif kind == Z_FIRST:
            src, dst, dev = part_z.at[k, ozl], first_in, zl_dev
        elif kind > Z_FIRST:
            dest, dst, dev = {
                Z_FAR: (x_far, z_far_in, xa_dev),
                Z_MID: (x_ahead, z_mid_in, xa_dev),
                Z_NEAR: (x_behind, z_near_in, xb_dev),
            }[kind]
            src = part_z.at[k, zl, dest]
        else:
            dest, dst, dev = {
                FAR: (x_far, far_in, xa_dev),
                MID: (x_ahead, mid_in, xa_dev),
                NEAR: (x_behind, near_in, xb_dev),
            }[kind]
            src = part.at[k, pl.ds(dest * 2, 2)]
        return pltpu.make_async_remote_copy(
            src_ref=src, dst_ref=dst.at[k], send_sem=rs_send.at[kind], recv_sem=rs_recv.at[k, kind],
            device_id=dev, device_id_type=MESH,
        )

    def f32(value):
        return value.astype(jnp.float32)

    def pair_sum(k, dest):
        return f32(part_z[k, zl, dest]) + f32(first_in[k, dest])

    def reduce_first(k):
        rs_copy(k, Z_FIRST).wait_recv()
        for kind, dest in ((Z_FAR, x_far), (Z_NEAR, x_behind)):
            part_z[k, zl, dest] = pair_sum(k, dest).astype(jnp.bfloat16)
            rs_copy(k, kind).start()

    def reduce_mid(k):
        rs_copy(k, FAR).wait_recv()
        for lo in range(2):
            dest = x_ahead * 2 + lo
            part[k, dest] = (f32(part[k, dest]) + f32(far_in[k, lo])).astype(jnp.bfloat16)
        rs_copy(k, MID).start()

    def reduce_z_mid(k):
        rs_copy(k, Z_FAR).wait_recv()
        total = pair_sum(k, x_ahead) + f32(z_far_in[k])
        part_z[k, zl, x_ahead] = total.astype(jnp.bfloat16)
        rs_copy(k, Z_MID).start()

    def reduce_z(k):
        rs_copy(k, NEAR).wait_recv()
        rs_copy(k, MID).wait_recv()
        dest = x * 2 + ozl
        total = f32(part[k, dest]) + f32(mid_in[k, ozl]) + f32(near_in[k, ozl])
        part[k, dest] = total.astype(jnp.bfloat16)
        rs_copy(k, ZSUM).start()

    def finish(k):
        for kind in (Z_MID, Z_NEAR, ZSUM):
            rs_copy(k, kind).wait_recv()
        last = wide - columns
        for half in range(2):
            out_rows = pl.ds(pl.multiple_of(half * tokens + k * piece, piece), piece)
            total = f32(part[k, x * 2 + zl, half]) + f32(mid_in[k, zl, half])
            total = total + f32(near_in[k, zl, half]) + f32(z_in[k, half])
            stream = f32(res_ref[out_rows])
            out_ref[out_rows, :columns] = (stream + total[:, :columns]).astype(jnp.bfloat16)
            if last:
                out_ref[out_rows, columns:wide] = (stream[:, :last] + total[:, columns:]).astype(jnp.bfloat16)
            total = f32(part_z[k, zl, x, half]) + f32(first_in[k, x, half])
            total = total + f32(z_mid_in[k, half]) + f32(z_near_in[k, half])
            out_ref[out_rows, wide:] = (stream[:, last:] + total).astype(jnp.bfloat16)
        for copy in out_copies(k):
            copy.start()

    def out_copies(k):
        copies = []
        for half in range(2):
            rows = pl.ds(pl.multiple_of(half * tokens + k * piece, piece), piece)
            copies.append(pltpu.make_async_copy(out_ref.at[rows], out_hbm.at[rows], out_sem.at[k, half]))
        return copies

    def make_hidden(k):
        rows = pl.ds(pl.multiple_of(k * piece, piece), piece)
        gate, up = f32(gate_buf[rows]), f32(up_buf[rows])
        hid[k, core, y * 2 + zh] = (gate / (1.0 + jnp.exp(-gate)) * up).astype(jnp.bfloat16)

    for copy in in_copies[:2]:
        copy.wait()
    make_hidden(0)
    pl.semaphore_wait(barrier, 7)
    across_z(0)
    ag(single(0, y, zh), 0, Y_AHEAD, ya_dev).start()
    ag(single(0, y, zh), 0, Y_BEHIND, yb_dev).start()

    for copy in in_copies[2:4]:
        copy.wait()

    @pl.loop(1, CHUNKS)
    def _(k):
        make_hidden(k)
        across_z(k)

    ag(single(0, y, oz), 0, ZP, zp_dev).wait_recv()
    ag(single(0, y, oz), 0, FIRST_OTHER, ya_dev).start()
    ag(single(0, y, oz), 0, Y_BEHIND, yb_dev).start()
    to_sibling(0, y)
    for copy in in_copies[4:]:
        copy.wait()
    factor_ref[...] = STEP_SIZE * jnp.exp2(expo_ref[...].astype(jnp.float32))

    @pl.loop(0, w_tiles)
    def _(i):
        for copy in w_copies(i):
            copy.wait()
        for g in range(W_ROWS // group):
            rows = pl.ds(pl.multiple_of(i * W_ROWS + g * group, group), group)
            factor = factor_ref[pl.ds(i * (W_ROWS // group) + g, 1)]
            left, right = slice(0, columns), slice(columns, 2 * columns)
            base = f32(weight[rows, left])
            shift = factor * f32(weight[rows, right])
            weight[rows, left] = (base + shift).astype(jnp.bfloat16)
            weight[rows, right] = (base - shift).astype(jnp.bfloat16)

        @pl.when(i == W_AT[0])
        def _():
            ag(single(0, y_behind, zh), 0, Y_AHEAD, ya_dev).wait_recv()
            ag(single(0, y_behind, zh), 0, Y_FAR, ya_dev).start()

        @pl.when(i == W_AT[1])
        def _():
            ag(single(0, y_behind, oz), 0, FIRST_OTHER, ya_dev).wait_recv()
            ag(single(0, y_behind, oz), 0, Y_FAR, ya_dev).start()
            along_y(1)
            to_sibling(0, y_behind)
            ag(pair(0, y_ahead), 0, Y_BEHIND, yb_dev).wait_recv()
            to_sibling(0, y_ahead)
            along_y(2)

    last_to_sibling(0)

    @pl.loop(0, CHUNKS)
    def _(k):
        all_here(k)
        more = k + 1 < CHUNKS

        def product(span):
            lhs = hid[k].reshape(2 * part.shape[1] * piece, depth)
            out = jnp.dot(lhs, weight[:, slice(*span)], preferred_element_type=jnp.float32)
            return out.astype(jnp.bfloat16).reshape(2, part.shape[1], piece, span[1] - span[0])

        for n, span in enumerate(X_TILES):
            out = product(span)
            for half in range(2):
                part[k, :, half, :, slice(*span)] = out[half]

            if n == FIRST_AT:
                @pl.when(k == 0)
                def _():
                    onward(1)
                    along_y(3)

        rs_copy(k, FAR).start()
        rs_copy(k, NEAR).start()
        @pl.when(k + 2 < CHUNKS)
        def _():
            onward(k + 2)

        @pl.when(k + 4 < CHUNKS)
        def _():
            along_y(k + 4)

        out = product(Z_TILE)
        for half in range(2):
            for dest in range(part.shape[1]):
                part_z[k, dest % 2, dest // 2, half] = out[half, dest]
        rs_copy(k, Z_FIRST).start()

        @pl.when(more)
        def _():
            last_to_sibling(k + 1)

        @pl.when(k >= 1)
        def _():
            reduce_first(k - 1)

        @pl.when(k >= 1)
        def _():
            reduce_mid(k - 1)

        @pl.when(k >= 2)
        def _():
            reduce_z_mid(k - 2)
            reduce_z(k - 2)

        @pl.when(k >= 3)
        def _():
            finish(k - 3)

    reduce_mid(CHUNKS - 1)
    reduce_z_mid(CHUNKS - 2)
    reduce_z(CHUNKS - 2)
    reduce_first(CHUNKS - 1)
    finish(CHUNKS - 3)
    reduce_z(CHUNKS - 1)
    reduce_z_mid(CHUNKS - 1)
    finish(CHUNKS - 2)
    finish(CHUNKS - 1)

    @pl.loop(0, CHUNKS)
    def _(k):
        for copy in out_copies(k):
            copy.wait()

    def sent(src, sem):
        pltpu.make_async_remote_copy(
            src_ref=src, dst_ref=src, send_sem=sem, recv_sem=ag_recv.at[0, 0],
            device_id=sib_dev, device_id_type=MESH,
        ).wait_send()

    sent(hid.at[:, 0, pl.ds(0, 7)], ag_send.at[0])
    sent(hid.at[:, 0], ag_send.at[1])
    for kind in (FAR, MID, NEAR):
        sent(part.at[:, pl.ds(0, 2)], rs_send.at[kind])
    sent(part.at[:, 0], rs_send.at[ZSUM])
    sent(part_z.at[:, 0], rs_send.at[Z_FIRST])
    for kind in (Z_FAR, Z_MID, Z_NEAR):
        sent(part_z.at[:, 0, 0], rs_send.at[kind])


def on_device(gate_pre, up_pre, residual, base_weight, perturb, exponents):
    tokens, depth = gate_pre.shape
    columns = base_weight.shape[1]
    n_col, n_row = 16, 8
    piece = tokens // CHUNKS
    wide, wide_z = Z_TILE[0], Z_TILE[1] - Z_TILE[0]
    bf16 = jnp.bfloat16
    out = jax.ShapeDtypeStruct((residual.shape[0], 2 * columns), bf16)
    any_spec = pl.BlockSpec(memory_space=pl.ANY)
    block, block_z = (2, piece, wide), (2, piece, wide_z)
    both = pl.pallas_call(
        kernel,
        out_shape=out,
        in_specs=[any_spec] * 6,
        out_specs=any_spec,
        scratch_shapes=[
            pltpu.VMEM((tokens, depth), bf16),
            pltpu.VMEM((tokens, depth), bf16),
            pltpu.VMEM(residual.shape, bf16),
            pltpu.VMEM(exponents.shape, jnp.int32),
            pltpu.VMEM(out.shape, bf16),
            pltpu.VMEM(exponents.shape, jnp.float32),
            pltpu.VMEM((CHUNKS, 2, n_col // 2, piece, depth), bf16),
            pltpu.VMEM((depth, 2 * columns), bf16),
            pltpu.VMEM((CHUNKS, n_row, *block), bf16),
            pltpu.VMEM((CHUNKS, 2, n_row // 2, *block_z), bf16),
            pltpu.VMEM((CHUNKS, 2, *block), bf16),
            pltpu.VMEM((CHUNKS, 2, *block), bf16),
            pltpu.VMEM((CHUNKS, 2, *block), bf16),
            pltpu.VMEM((CHUNKS, *block), bf16),
            pltpu.VMEM((CHUNKS, n_row // 2, *block_z), bf16),
            pltpu.VMEM((CHUNKS, *block_z), bf16),
            pltpu.VMEM((CHUNKS, *block_z), bf16),
            pltpu.VMEM((CHUNKS, *block_z), bf16),
            pltpu.SemaphoreType.DMA((6,)),
            pltpu.SemaphoreType.DMA((CHUNKS, 2)),
            pltpu.SemaphoreType.DMA((depth // W_ROWS, 2)),
            pltpu.SemaphoreType.DMA((2,)),
            pltpu.SemaphoreType.DMA((CHUNKS, 6)),
            pltpu.SemaphoreType.DMA((8,)),
            pltpu.SemaphoreType.DMA((CHUNKS, 8)),
        ],
        compiler_params=pltpu.CompilerParams(
            collective_id=0, has_side_effects=True, vmem_limit_bytes=60 * 1024 * 1024
        ),
        cost_estimate=pl.CostEstimate(
            flops=2 * n_col * tokens * depth * 2 * columns,
            bytes_accessed=4 * depth * columns,
            transcendentals=tokens * depth,
        ),
    )(gate_pre, up_pre, residual, base_weight, perturb, exponents)
    return both[:, :columns], both[:, columns:]


def solution(mesh):
    spec = P("row", "col")
    turned = P("col", "row")
    return jax.shard_map(
        on_device,
        mesh=mesh,
        in_specs=(turned, turned, spec, spec, spec, spec),
        out_specs=(spec, spec),
        check_vma=False,
    )
```

```python
import jax
import jax.numpy as jnp
from jax import lax
from jax.experimental import pallas as pl
from jax.experimental.pallas import tpu as pltpu
from jax.sharding import PartitionSpec as P

MESH = pl.DeviceIdType.MESH
STEP_SIZE = 0.25
CHUNKS = 8
X_TILES = ((0, 640), (640, 1152))
Z_TILE = (1152, 2048)
W_ROWS = 256
FIRST_AT = 0
W_AT = (5, 9)
ZP, Y_AHEAD, Y_BEHIND, Y_FAR, SIB, FIRST_OTHER = range(6)
FAR, MID, NEAR, ZSUM, Z_FIRST, Z_FAR, Z_MID, Z_NEAR = range(8)


def kernel(
    gate_hbm, up_hbm, res_hbm, base_hbm, pert_hbm, expo_hbm,
    out_hbm,
    gate_buf, up_buf, res_ref, expo_ref, out_ref, factor_ref, hid, weight, part, part_z,
    far_in, mid_in, near_in, z_in, first_in, z_far_in, z_mid_in, z_near_in,
    in_sem, out_sem, w_sem, ag_send, ag_recv, rs_send, rs_recv,
):
    tokens, depth = gate_buf.shape
    piece = tokens // CHUNKS
    columns = weight.shape[1] // 2
    wide, wide_z = part.shape[-1], part_z.shape[-1]
    w_tiles = depth // W_ROWS
    group = depth // expo_ref.shape[0]

    row, col = lax.axis_index("row"), lax.axis_index("col")
    x, zl = row // 2, row % 2
    y, zh, core = col // 4, (col // 2) % 2, col % 2
    step = 2 * core + 3
    back = 5 - 2 * core
    x_ahead, x_behind, x_far = (x + step) % 4, (x + back) % 4, (x + 2) % 4
    y_ahead, y_behind, y_far = (y + step) % 4, (y + back) % 4, (y + 2) % 4
    oz, oc, ozl = 1 - zh, 1 - core, 1 - zl

    def col_of(y_, zh_, core_):
        return y_ * 4 + zh_ * 2 + core_

    zp_dev = (row, col_of(y, oz, core))
    ya_dev, yb_dev = (row, col_of(y_ahead, zh, core)), (row, col_of(y_behind, zh, core))
    sib_dev = (row, col_of(y, zh, oc))
    xa_dev, xb_dev = (x_ahead * 2 + zl, col), (x_behind * 2 + zl, col)
    zl_dev = (x * 2 + ozl, col)

    head, rest = pl.ds(0, piece), pl.ds(piece, tokens - piece)
    in_copies = [
        pltpu.make_async_copy(gate_hbm.at[head], gate_buf.at[head], in_sem.at[0]),
        pltpu.make_async_copy(up_hbm.at[head], up_buf.at[head], in_sem.at[1]),
        pltpu.make_async_copy(gate_hbm.at[rest], gate_buf.at[rest], in_sem.at[2]),
        pltpu.make_async_copy(up_hbm.at[rest], up_buf.at[rest], in_sem.at[3]),
        pltpu.make_async_copy(expo_hbm, expo_ref, in_sem.at[4]),
        pltpu.make_async_copy(res_hbm, res_ref, in_sem.at[5]),
    ]

    def w_copies(i):
        rows = pl.ds(pl.multiple_of(i * W_ROWS, W_ROWS), W_ROWS)
        return [
            pltpu.make_async_copy(
                source.at[rows], weight.at[rows, pl.ds(j * columns, columns)], w_sem.at[i, j]
            )
            for j, source in enumerate((base_hbm, pert_hbm))
        ]

    barrier = pltpu.get_barrier_semaphore()
    for dev in (zp_dev, ya_dev, yb_dev, sib_dev, xa_dev, xb_dev, zl_dev):
        pl.semaphore_signal(barrier, inc=1, device_id=dev, device_id_type=MESH)
    for copy in in_copies:
        copy.start()

    @pl.loop(0, w_tiles)
    def _(i):
        for copy in w_copies(i):
            copy.start()

    def ag(src, k, kind, dev):
        return pltpu.make_async_remote_copy(
            src_ref=src, dst_ref=src, send_sem=ag_send.at[kind == SIB and 1 or 0], recv_sem=ag_recv.at[k, kind],
            device_id=dev, device_id_type=MESH,
        )

    def single(k, y_, zh_):
        return hid.at[k, core, y_ * 2 + zh_]

    def pair(k, y_):
        return hid.at[k, core, pl.ds(y_ * 2, 2)]

    def to_sibling(k, y_):
        ag(pair(k, y_), k, SIB, sib_dev).start()

    def across_z(k):
        ag(single(k, y, zh), k, ZP, zp_dev).start()

    def along_y(k):
        ag(single(k, y, oz), k, ZP, zp_dev).wait_recv()
        ag(pair(k, y), k, Y_AHEAD, ya_dev).start()
        ag(pair(k, y), k, Y_BEHIND, yb_dev).start()
        to_sibling(k, y)

    def onward(k):
        ag(pair(k, y_behind), k, Y_AHEAD, ya_dev).wait_recv()
        ag(pair(k, y_behind), k, Y_FAR, ya_dev).start()
        to_sibling(k, y_behind)
        ag(pair(k, y_ahead), k, Y_BEHIND, yb_dev).wait_recv()
        to_sibling(k, y_ahead)

    def last_to_sibling(k):
        ag(pair(k, y_far), k, Y_FAR, ya_dev).wait_recv()
        to_sibling(k, y_far)

    def all_here(k):
        ag(hid.at[k, oc], k, SIB, sib_dev).wait_recv()

    def rs_copy(k, kind):
        if kind == ZSUM:
            src, dst, dev = part.at[k, x * 2 + ozl], z_in, zl_dev
        elif kind == Z_FIRST:
            src, dst, dev = part_z.at[k, ozl], first_in, zl_dev
        elif kind > Z_FIRST:
            dest, dst, dev = {
                Z_FAR: (x_far, z_far_in, xa_dev),
                Z_MID: (x_ahead, z_mid_in, xa_dev),
                Z_NEAR: (x_behind, z_near_in, xb_dev),
            }[kind]
            src = part_z.at[k, zl, dest]
        else:
            dest, dst, dev = {
                FAR: (x_far, far_in, xa_dev),
                MID: (x_ahead, mid_in, xa_dev),
                NEAR: (x_behind, near_in, xb_dev),
            }[kind]
            src = part.at[k, pl.ds(dest * 2, 2)]
        return pltpu.make_async_remote_copy(
            src_ref=src, dst_ref=dst.at[k], send_sem=rs_send.at[kind], recv_sem=rs_recv.at[k, kind],
            device_id=dev, device_id_type=MESH,
        )

    def f32(value):
        return value.astype(jnp.float32)

    def pair_sum(k, dest):
        return f32(part_z[k, zl, dest]) + f32(first_in[k, dest])

    def reduce_first(k):
        rs_copy(k, Z_FIRST).wait_recv()
        for kind, dest in ((Z_FAR, x_far), (Z_NEAR, x_behind)):
            part_z[k, zl, dest] = pair_sum(k, dest).astype(jnp.bfloat16)
            rs_copy(k, kind).start()

    def reduce_mid(k):
        rs_copy(k, FAR).wait_recv()
        for lo in range(2):
            dest = x_ahead * 2 + lo
            part[k, dest] = (f32(part[k, dest]) + f32(far_in[k, lo])).astype(jnp.bfloat16)
        rs_copy(k, MID).start()

    def reduce_z_mid(k):
        rs_copy(k, Z_FAR).wait_recv()
        total = pair_sum(k, x_ahead) + f32(z_far_in[k])
        part_z[k, zl, x_ahead] = total.astype(jnp.bfloat16)
        rs_copy(k, Z_MID).start()

    def reduce_z(k):
        rs_copy(k, NEAR).wait_recv()
        rs_copy(k, MID).wait_recv()
        dest = x * 2 + ozl
        total = f32(part[k, dest]) + f32(mid_in[k, ozl]) + f32(near_in[k, ozl])
        part[k, dest] = total.astype(jnp.bfloat16)
        rs_copy(k, ZSUM).start()

    def finish(k):
        for kind in (Z_MID, Z_NEAR, ZSUM):
            rs_copy(k, kind).wait_recv()
        last = wide - columns
        for half in range(2):
            out_rows = pl.ds(pl.multiple_of(half * tokens + k * piece, piece), piece)
            total = f32(part[k, x * 2 + zl, half]) + f32(mid_in[k, zl, half])
            total = total + f32(near_in[k, zl, half]) + f32(z_in[k, half])
            stream = f32(res_ref[out_rows])
            out_ref[out_rows, :columns] = (stream + total[:, :columns]).astype(jnp.bfloat16)
            if last:
                out_ref[out_rows, columns:wide] = (stream[:, :last] + total[:, columns:]).astype(jnp.bfloat16)
            total = f32(part_z[k, zl, x, half]) + f32(first_in[k, x, half])
            total = total + f32(z_mid_in[k, half]) + f32(z_near_in[k, half])
            out_ref[out_rows, wide:] = (stream[:, last:] + total).astype(jnp.bfloat16)
        for copy in out_copies(k):
            copy.start()

    def out_copies(k):
        copies = []
        for half in range(2):
            rows = pl.ds(pl.multiple_of(half * tokens + k * piece, piece), piece)
            copies.append(pltpu.make_async_copy(out_ref.at[rows], out_hbm.at[rows], out_sem.at[k, half]))
        return copies

    def make_hidden(k):
        rows = pl.ds(pl.multiple_of(k * piece, piece), piece)
        gate, up = f32(gate_buf[rows]), f32(up_buf[rows])
        hid[k, core, y * 2 + zh] = (gate / (1.0 + jnp.exp(-gate)) * up).astype(jnp.bfloat16)

    for copy in in_copies[:2]:
        copy.wait()
    make_hidden(0)
    pl.semaphore_wait(barrier, 7)
    across_z(0)
    ag(single(0, y, zh), 0, Y_AHEAD, ya_dev).start()
    ag(single(0, y, zh), 0, Y_BEHIND, yb_dev).start()

    for copy in in_copies[2:4]:
        copy.wait()

    @pl.loop(1, CHUNKS)
    def _(k):
        make_hidden(k)
        across_z(k)

    ag(single(0, y, oz), 0, ZP, zp_dev).wait_recv()
    ag(single(0, y, oz), 0, FIRST_OTHER, ya_dev).start()
    ag(single(0, y, oz), 0, Y_BEHIND, yb_dev).start()
    to_sibling(0, y)
    for copy in in_copies[4:]:
        copy.wait()
    factor_ref[...] = STEP_SIZE * jnp.exp2(expo_ref[...].astype(jnp.float32))

    @pl.loop(0, w_tiles)
    def _(i):
        for copy in w_copies(i):
            copy.wait()
        for g in range(W_ROWS // group):
            rows = pl.ds(pl.multiple_of(i * W_ROWS + g * group, group), group)
            factor = factor_ref[pl.ds(i * (W_ROWS // group) + g, 1)]
            left, right = slice(0, columns), slice(columns, 2 * columns)
            base = f32(weight[rows, left])
            shift = factor * f32(weight[rows, right])
            weight[rows, left] = (base + shift).astype(jnp.bfloat16)
            weight[rows, right] = (base - shift).astype(jnp.bfloat16)

        @pl.when(i == W_AT[0])
        def _():
            ag(single(0, y_behind, zh), 0, Y_AHEAD, ya_dev).wait_recv()
            ag(single(0, y_behind, zh), 0, Y_FAR, ya_dev).start()

        @pl.when(i == W_AT[1])
        def _():
            ag(single(0, y_behind, oz), 0, FIRST_OTHER, ya_dev).wait_recv()
            ag(single(0, y_behind, oz), 0, Y_FAR, ya_dev).start()
            along_y(1)
            to_sibling(0, y_behind)
            ag(pair(0, y_ahead), 0, Y_BEHIND, yb_dev).wait_recv()
            to_sibling(0, y_ahead)
            along_y(2)

    last_to_sibling(0)

    @pl.loop(0, CHUNKS)
    def _(k):
        all_here(k)
        more = k + 1 < CHUNKS

        def product(span):
            lhs = hid[k].reshape(2 * part.shape[1] * piece, depth)
            out = jnp.dot(lhs, weight[:, slice(*span)], preferred_element_type=jnp.float32)
            return out.astype(jnp.bfloat16).reshape(2, part.shape[1], piece, span[1] - span[0])

        for n, span in enumerate(X_TILES):
            out = product(span)
            for half in range(2):
                part[k, :, half, :, slice(*span)] = out[half]

            if n == FIRST_AT:
                @pl.when(k == 0)
                def _():
                    onward(1)
                    along_y(3)

        rs_copy(k, FAR).start()
        rs_copy(k, NEAR).start()
        @pl.when(k + 2 < CHUNKS)
        def _():
            onward(k + 2)

        @pl.when(k + 4 < CHUNKS)
        def _():
            along_y(k + 4)

        out = product(Z_TILE)
        for half in range(2):
            for dest in range(part.shape[1]):
                part_z[k, dest % 2, dest // 2, half] = out[half, dest]
        rs_copy(k, Z_FIRST).start()

        @pl.when(k >= 1)
        def _():
            reduce_mid(k - 1)

        @pl.when(more)
        def _():
            last_to_sibling(k + 1)

        @pl.when(k >= 1)
        def _():
            reduce_first(k - 1)

        @pl.when(k >= 2)
        def _():
            reduce_z_mid(k - 2)
            reduce_z(k - 2)

        @pl.when(k >= 3)
        def _():
            finish(k - 3)

    reduce_mid(CHUNKS - 1)
    reduce_z_mid(CHUNKS - 2)
    reduce_z(CHUNKS - 2)
    reduce_first(CHUNKS - 1)
    finish(CHUNKS - 3)
    reduce_z(CHUNKS - 1)
    reduce_z_mid(CHUNKS - 1)
    finish(CHUNKS - 2)
    finish(CHUNKS - 1)

    @pl.loop(0, CHUNKS)
    def _(k):
        for copy in out_copies(k):
            copy.wait()

    def sent(src, sem):
        pltpu.make_async_remote_copy(
            src_ref=src, dst_ref=src, send_sem=sem, recv_sem=ag_recv.at[0, 0],
            device_id=sib_dev, device_id_type=MESH,
        ).wait_send()

    sent(hid.at[:, 0, pl.ds(0, 7)], ag_send.at[0])
    sent(hid.at[:, 0], ag_send.at[1])
    for kind in (FAR, MID, NEAR):
        sent(part.at[:, pl.ds(0, 2)], rs_send.at[kind])
    sent(part.at[:, 0], rs_send.at[ZSUM])
    sent(part_z.at[:, 0], rs_send.at[Z_FIRST])
    for kind in (Z_FAR, Z_MID, Z_NEAR):
        sent(part_z.at[:, 0, 0], rs_send.at[kind])


def on_device(gate_pre, up_pre, residual, base_weight, perturb, exponents):
    tokens, depth = gate_pre.shape
    columns = base_weight.shape[1]
    n_col, n_row = 16, 8
    piece = tokens // CHUNKS
    wide, wide_z = Z_TILE[0], Z_TILE[1] - Z_TILE[0]
    bf16 = jnp.bfloat16
    out = jax.ShapeDtypeStruct((residual.shape[0], 2 * columns), bf16)
    any_spec = pl.BlockSpec(memory_space=pl.ANY)
    block, block_z = (2, piece, wide), (2, piece, wide_z)
    both = pl.pallas_call(
        kernel,
        out_shape=out,
        in_specs=[any_spec] * 6,
        out_specs=any_spec,
        scratch_shapes=[
            pltpu.VMEM((tokens, depth), bf16),
            pltpu.VMEM((tokens, depth), bf16),
            pltpu.VMEM(residual.shape, bf16),
            pltpu.VMEM(exponents.shape, jnp.int32),
            pltpu.VMEM(out.shape, bf16),
            pltpu.VMEM(exponents.shape, jnp.float32),
            pltpu.VMEM((CHUNKS, 2, n_col // 2, piece, depth), bf16),
            pltpu.VMEM((depth, 2 * columns), bf16),
            pltpu.VMEM((CHUNKS, n_row, *block), bf16),
            pltpu.VMEM((CHUNKS, 2, n_row // 2, *block_z), bf16),
            pltpu.VMEM((CHUNKS, 2, *block), bf16),
            pltpu.VMEM((CHUNKS, 2, *block), bf16),
            pltpu.VMEM((CHUNKS, 2, *block), bf16),
            pltpu.VMEM((CHUNKS, *block), bf16),
            pltpu.VMEM((CHUNKS, n_row // 2, *block_z), bf16),
            pltpu.VMEM((CHUNKS, *block_z), bf16),
            pltpu.VMEM((CHUNKS, *block_z), bf16),
            pltpu.VMEM((CHUNKS, *block_z), bf16),
            pltpu.SemaphoreType.DMA((6,)),
            pltpu.SemaphoreType.DMA((CHUNKS, 2)),
            pltpu.SemaphoreType.DMA((depth // W_ROWS, 2)),
            pltpu.SemaphoreType.DMA((2,)),
            pltpu.SemaphoreType.DMA((CHUNKS, 6)),
            pltpu.SemaphoreType.DMA((8,)),
            pltpu.SemaphoreType.DMA((CHUNKS, 8)),
        ],
        compiler_params=pltpu.CompilerParams(
            collective_id=0, has_side_effects=True, vmem_limit_bytes=60 * 1024 * 1024
        ),
        cost_estimate=pl.CostEstimate(
            flops=2 * n_col * tokens * depth * 2 * columns,
            bytes_accessed=4 * depth * columns,
            transcendentals=tokens * depth,
        ),
    )(gate_pre, up_pre, residual, base_weight, perturb, exponents)
    return both[:, :columns], both[:, columns:]


def solution(mesh):
    spec = P("row", "col")
    turned = P("col", "row")
    return jax.shard_map(
        on_device,
        mesh=mesh,
        in_specs=(turned, turned, spec, spec, spec, spec),
        out_specs=(spec, spec),
        check_vma=False,
    )
```
